32 devices in a mesh: rep: 4 (over x, core), fsdp: 8 (over z, y).
Axes of the slice: x: 2, y: 2, z: 4, core: 2. Of those that a mesh axis runs over, the one named last changes fastest.
Arguments:
- tokens: bfloat16 [8192, 2048], P(('rep', 'fsdp')), may hold values from -6 to 6
- query_weight: bfloat16 [2048, 2048], P('fsdp'), may hold values from -0.125 to 0.125
- key_weight: bfloat16 [2048, 2048], P('fsdp'), may hold values from -0.125 to 0.125
- value_weight: bfloat16 [2048, 2048], P('fsdp'), may hold values from -0.125 to 0.125
- query_norm: bfloat16 [2048], P('fsdp'), may hold values from 0.25 to 1.75
- key_norm: bfloat16 [2048], P('fsdp'), may hold values from 0.25 to 1.75
- output_weight: bfloat16 [2048, 2048], P('fsdp'), may hold values from -0.125 to 0.125
- mixer_norm: bfloat16 [2048], P('fsdp'), may hold values from 0.25 to 1.75
- gate_weight: bfloat16 [2048, 8192], P(None, 'fsdp'), may hold values from -0.125 to 0.125
- up_weight: bfloat16 [2048, 8192], P(None, 'fsdp'), may hold values from -0.125 to 0.125
- down_weight: bfloat16 [2048, 8192], P(None, 'fsdp'), may hold values from -0.0625 to 0.0625
- feeder_norm: bfloat16 [2048], P('fsdp'), may hold values from 0.25 to 1.75
- piece_starts: int32 [4, 2], replicated, may hold values from 0 to 1792, as said below
- cotangent: bfloat16 [8192, 2048], P(('rep', 'fsdp')), may hold values from -6 to 6
Outputs:
- result: bfloat16 [8192, 2048], P(('rep', 'fsdp'))
- gradient_tokens: bfloat16 [8192, 2048], P(('rep', 'fsdp'))
- gradient_query: float32 [2048, 2048], P('fsdp')
- gradient_key: float32 [2048, 2048], P('fsdp')
- gradient_value: float32 [2048, 2048], P('fsdp')
- gradient_querynorm: float32 [2048], P('fsdp')
- gradient_keynorm: float32 [2048], P('fsdp')
- gradient_output: float32 [2048, 2048], P('fsdp')
- gradient_mixernorm: float32 [2048], P('fsdp')
- gradient_gate: float32 [2048, 8192], P(None, 'fsdp')
- gradient_up: float32 [2048, 8192], P(None, 'fsdp')
- gradient_down: float32 [2048, 8192], P(None, 'fsdp')
- gradient_feedernorm: float32 [2048], P('fsdp')
The draws below stay inside these ranges and needn't reach their ends.
Inputs may be any that keep to these rules, and one draw needn't show every extreme that they name: `piece_starts`: each of the 4 sequences holds 2 pieces of 256 tokens; piece j of a sequence starts between j * 1024 and (j + 1) * 1024 - 256, so the pieces of a sequence never intersect. Positions count from the sequence's first token.
All inputs are finite; a program needn't handle non-finite values.
Results may differ from the reference program's by a relative error of at most 0.022.
Values may be sent and summed in bfloat16 or wider, within the bound.
No kernel may reach another device: no remote copies, remote signals or barrier semaphores. Data moves between devices by JAX's collectives and lax.ppermute only.
A program may use at most 832 MiB of HBM per device.

```python
import jax
import jax.numpy as jnp
from jax import lax

D = 2048
HEADS = 16
HEAD_DIM = 128
FF = 8192
SEQ = 2048
PIECE = 256
PIECES = 2
TOKENS = 8192
SEQS = 4


def draw_piece_starts(key, part):
    zone = SEQ // PIECES
    shifts = jax.random.randint(key, (SEQS, PIECES), 0, zone - PIECE + 1, dtype=jnp.int32)
    row_ids = jnp.arange(SEQS, dtype=jnp.int32)[:, None]
    col_ids = jnp.arange(PIECES, dtype=jnp.int32)[None, :]
    shifts = jnp.where((row_ids == 0) & (col_ids == 0), 0, shifts)
    shifts = jnp.where((row_ids == 0) & (col_ids == PIECES - 1), zone - PIECE, shifts)
    return (col_ids * zone + shifts).astype(jnp.int32)


def with_spikes(array, rng, source, target, blocks, factor):
    def block_of(position):
        return (jnp.arange(array.shape[position]) // (array.shape[position] // blocks)).reshape((-1,) + (1,) * (array.ndim - 1 - position))

    one_side = jax.random.permutation(rng, blocks)[block_of(target)]
    far = (block_of(target) + blocks // 2) % blocks
    return jnp.where((block_of(source) == one_side) | (block_of(source) == far), factor * array, array)


def block_levels(stream_key, dims, pieces, smallest, largest):
    level, own = 1.0, jax.random.fold_in(stream_key, 6)
    for axis_at, parts in pieces:
        steps = jnp.exp(jax.random.uniform(jax.random.fold_in(own, axis_at), (parts,), jnp.float32, smallest / len(pieces), largest / len(pieces)))
        level = level * jnp.repeat(steps, dims[axis_at] // parts).reshape([-1 if axis == axis_at else 1 for axis in range(len(dims))])
    return level


def gaussian(rng, extent, deviation, most, cuts=(), held_as=jnp.bfloat16):
    entries = deviation * jax.random.normal(rng, extent, jnp.float32)
    if cuts:
        entries = entries * block_levels(rng, extent, cuts, -0.22, 0.18)
    return jnp.clip(entries, -most, most).astype(held_as)


def gaussian_with(own_key, shape, width, bound, shards, heavy, kind=jnp.bfloat16):
    values = width * jax.random.normal(own_key, shape, jnp.float32)
    if shards:
        values = values * block_levels(own_key, shape, shards, -0.22, 0.18)
    return jnp.clip(with_spikes(values, jax.random.fold_in(own_key, 3), *heavy), -bound, bound).astype(kind)


def setup_inputs(seed: int = 0) -> dict:
    key_list = jax.random.split(jax.random.key(seed), 15)
    return {
        "tokens": gaussian_with(key_list[0], (TOKENS, D), 1.0, 6.0, ((0, 32),), (0, 1, 32, 2.75)),
        "query_weight": gaussian(key_list[1], (D, D), D ** -0.5, 0.125, ((0, 8),)),
        "key_weight": gaussian(key_list[2], (D, D), D ** -0.5, 0.125, ((0, 8),)),
        "value_weight": gaussian(key_list[3], (D, D), D ** -0.5, 0.125, ((0, 8),)),
        "query_norm": jnp.clip(1.0 + 0.15 * jax.random.normal(key_list[4], (D,), jnp.float32), 0.25, 1.75).astype(jnp.bfloat16),
        "key_norm": jnp.clip(1.0 + 0.15 * jax.random.normal(key_list[5], (D,), jnp.float32), 0.25, 1.75).astype(jnp.bfloat16),
        "output_weight": gaussian(key_list[6], (D, D), D ** -0.5, 0.125, ((0, 8),)),
        "mixer_norm": jnp.clip(1.0 + 0.15 * jax.random.normal(key_list[7], (D,), jnp.float32), 0.25, 1.75).astype(jnp.bfloat16),
        "gate_weight": gaussian(key_list[8], (D, FF), D ** -0.5, 0.125, ((1, 8),)),
        "up_weight": gaussian(key_list[9], (D, FF), D ** -0.5, 0.125, ((1, 8),)),
        "down_weight": gaussian(key_list[10], (D, FF), FF ** -0.5, 0.0625, ((1, 8),)),
        "feeder_norm": jnp.clip(1.0 + 0.15 * jax.random.normal(key_list[11], (D,), jnp.float32), 0.25, 1.75).astype(jnp.bfloat16),
        "piece_starts": draw_piece_starts(jax.random.fold_in(key_list[14], 71), 0),
        "cotangent": gaussian_with(key_list[13], (TOKENS, D), 1.0, 6.0, ((0, 32),), (0, 1, 32, 2.75)),
    }


norm_epsilon = 1e-06
rope_base = 500000.0
masked_score = -1e+30

@jax.custom_vjp
def low(v):
    return lax.optimization_barrier(v.astype(jnp.bfloat16)).astype(jnp.float32)

@jax.custom_vjp
def low_back(v):
    return v

def low_keep(v):
    return (low(v), None)

def low_pass(kept, grad):
    return (grad,)

def back_keep(v):
    return (v, None)

def back_low(kept, grad):
    return (low(grad),)
low.defvjp(low_keep, low_pass)
low_back.defvjp(back_keep, back_low)

def product(first_op, second_op):
    return jnp.dot(first_op, second_op, precision=lax.Precision.HIGHEST, preferred_element_type=jnp.float32)

def scaled_norm(values, gain_row):
    factor = lax.rsqrt(lax.optimization_barrier(jnp.mean(values * values, axis=-1, keepdims=True)) + norm_epsilon)
    return values * factor * gain_row

def rope_tables(positions, head_dim):
    half_dim = head_dim // 2
    frequency = rope_base ** (-(jnp.arange(half_dim, dtype=jnp.float32) * (2.0 / head_dim)))
    angles = positions.astype(jnp.float32)[:, None] * frequency[None, :]
    return (jnp.cos(angles), jnp.sin(angles))

def rotate(values, cosine_table, sine_table, head_count):
    row_count = values.shape[0]
    shaped = values.reshape(row_count, head_count, 2, -1)
    first_half = shaped[:, :, 0]
    second_half = shaped[:, :, 1]
    cosine_part = cosine_table[:, None, :]
    sine_part = sine_table[:, None, :]
    turned = jnp.stack([first_half * cosine_part - second_half * sine_part, second_half * cosine_part + first_half * sine_part], axis=2)
    return turned.reshape(row_count, -1)

def piece_labels(places, piece_starts, piece_len, sequence_len):
    sequence_count, pieces_each = piece_starts.shape
    begins = (jnp.arange(sequence_count, dtype=jnp.int32)[:, None] * sequence_len + piece_starts).reshape(-1)
    inside = (places[:, None] >= begins[None, :]) & (places[:, None] < begins[None, :] + piece_len)
    labels = jnp.arange(1, sequence_count * pieces_each + 1, dtype=jnp.int32)
    return lax.optimization_barrier(jnp.sum(jnp.where(inside, labels[None, :], 0), axis=1)) - 1

def allowed_pairs(query_places, key_places, query_labels, key_labels, sequence_len):
    same = query_places[:, None] // sequence_len == key_places[None, :] // sequence_len
    causal = key_places[None, :] <= query_places[:, None]
    joint = (query_labels[:, None] == key_labels[None, :]) & (query_labels[:, None] >= 0)
    return same & (causal | joint)

def whole_layer(layer_input, weights, allowed, cosine_table, sine_table):
    query_weight, key_weight, value_weight, query_norm, key_norm, output_weight, mixer_norm, gate_weight, up_weight, down_weight, feeder_norm = weights
    row_count = layer_input.shape[0]
    query_pre = low_back(product(layer_input, query_weight))
    key_pre = low_back(product(layer_input, key_weight))
    values = low(low_back(product(layer_input, value_weight)))
    queries = low(rotate(scaled_norm(query_pre, query_norm), cosine_table, sine_table, HEADS))
    keys = low(rotate(scaled_norm(key_pre, key_norm), cosine_table, sine_table, HEADS))

    def by_heads(matrix):
        return matrix.reshape(row_count, HEADS, HEAD_DIM).transpose(1, 0, 2)

    def one_head(operands):
        head_query, head_key, head_value = operands
        scores = product(head_query, head_key.T) * HEAD_DIM ** (-0.5)
        scores = low_back(jnp.where(allowed, scores, masked_score))
        row_max = lax.optimization_barrier(jnp.max(scores, axis=1, keepdims=True))
        exponent = jnp.exp(scores - row_max)
        shares = low(exponent / lax.optimization_barrier(jnp.sum(exponent, axis=1, keepdims=True)))
        return product(shares, head_value)
    head_mixed = lax.map(jax.checkpoint(one_head), (by_heads(queries), by_heads(keys), by_heads(values)))
    mixed = low(low_back(head_mixed.transpose(1, 0, 2).reshape(row_count, -1)))
    branch_pre = low_back(product(mixed, output_weight))
    hidden = layer_input + scaled_norm(branch_pre, mixer_norm)
    hidden_low = low(hidden)
    gate_pre = low_back(product(hidden_low, gate_weight))
    up_pre = low_back(product(hidden_low, up_weight))
    inner = low(jax.nn.silu(gate_pre) * up_pre)
    down_pre = low_back(product(inner, down_weight.T))
    return hidden + scaled_norm(down_pre, feeder_norm)

def reference(tokens, query_weight, key_weight, value_weight, query_norm, key_norm, output_weight, mixer_norm, gate_weight, up_weight, down_weight, feeder_norm, piece_starts, cotangent):
    params = tuple((weight_arg.astype(jnp.float32) for weight_arg in (query_weight, key_weight, value_weight, query_norm, key_norm, output_weight, mixer_norm, gate_weight, up_weight, down_weight, feeder_norm)))
    positions = jnp.arange(SEQ, dtype=jnp.int32)
    cosine_table, sine_table = rope_tables(positions, HEAD_DIM)
    inputs = tokens.astype(jnp.float32).reshape(SEQS, SEQ, D)
    tangents = cotangent.astype(jnp.float32).reshape(SEQS, SEQ, D)

    def scan_step(totals, operands):
        sequence_id, sequence_rows, sequence_tangent = operands
        places = sequence_id * SEQ + positions
        labels = piece_labels(places, piece_starts, PIECE, SEQ)
        allowed = allowed_pairs(places, places, labels, labels, SEQ)

        def forward(layer_input, *weights):
            return whole_layer(layer_input, weights, allowed, cosine_table, sine_table)
        layer_result, pullback = jax.vjp(forward, sequence_rows, *params)
        gradients = pullback(sequence_tangent)
        totals = tuple((earlier + addend for earlier, addend in zip(totals, gradients[1:])))
        return (totals, (layer_result.astype(jnp.bfloat16), gradients[0].astype(jnp.bfloat16)))
    zero_grads = tuple((jnp.zeros_like(weight_arg) for weight_arg in params))
    totals, (results, input_grads) = lax.scan(scan_step, zero_grads, (jnp.arange(SEQS, dtype=jnp.int32), inputs, tangents))
    return (results.reshape(TOKENS, D), input_grads.reshape(TOKENS, D), totals[0], totals[1], totals[2], totals[3], totals[4], totals[5], totals[6], totals[7], totals[8], totals[9], totals[10])
```

```python
import functools

import jax
import jax.numpy as jnp
from jax import lax
from jax.experimental import pallas as pl
from jax.experimental.pallas import tpu as pltpu
from jax.sharding import PartitionSpec as P

HEADS = 16
HEAD_DIM = 128
SEQ = 2048
PIECE = 256
BLOCK = 512

norm_epsilon = 1e-06
rope_base = 500000.0
masked_score = -1e30
score_factor = HEAD_DIM ** (-0.5)
f32 = jnp.float32
bf16 = jnp.bfloat16


def matmul(a, b):
    return jnp.dot(a, b, preferred_element_type=f32)


def against(a, b):
    return lax.dot_general(a, b, (((1,), (1,)), ((), ())), preferred_element_type=f32)


def across(a, b):
    return lax.dot_general(a, b, (((0,), (0,)), ((), ())), preferred_element_type=f32)


def inverse_rms(values):
    return lax.rsqrt(jnp.mean(values * values, axis=-1, keepdims=True) + norm_epsilon)


def norm_backward(values, factor, gain_row, upstream):
    weighted = upstream * gain_row
    inner_mean = jnp.mean(weighted * values, axis=-1, keepdims=True)
    return factor * weighted - values * (factor * factor * factor) * inner_mean


def swapped(block, axis, bit):
    size = lax.axis_size(axis)
    return lax.ppermute(block, axis, [(i, i ^ bit) for i in range(size)])


def xor_sum(block, axis, size):
    bit = 1
    while bit < size:
        block = block + swapped(block, axis, bit)
        bit *= 2
    return block


def rep_sum(block):
    size = lax.axis_size("rep")
    me = lax.axis_index("rep")
    bits = []
    bit = 1
    while bit < size:
        bits.append(bit)
        bit *= 2
    for bit in bits:
        half = block.shape[0] // 2
        side = (me // bit) % 2
        keep = lax.dynamic_slice_in_dim(block, side * half, half, 0)
        send = lax.dynamic_slice_in_dim(block, (1 - side) * half, half, 0)
        got = swapped(send.astype(bf16), "rep", bit)
        block = keep.astype(f32) + got.astype(f32)
    block = block.astype(bf16)
    for bit in reversed(bits):
        side = (me // bit) % 2
        got = swapped(block, "rep", bit)
        block = jnp.where(
            side == 0, jnp.concatenate([block, got]), jnp.concatenate([got, block])
        )
    return block.astype(f32)


def piece_label(places, starts_ref):
    label = jnp.where((places >= starts_ref[0]) & (places < starts_ref[0] + PIECE), 1, 0)
    for j in range(1, starts_ref.shape[0]):
        inside = (places >= starts_ref[j]) & (places < starts_ref[j] + PIECE)
        label = jnp.where(inside, j + 1, label)
    return label


def allowed_block(starts_ref, query_start, query_count, key_start, key_count):
    query_places = query_start + lax.broadcasted_iota(jnp.int32, (query_count, 1), 0)
    key_places = key_start + lax.broadcasted_iota(jnp.int32, (1, key_count), 1)
    query_labels = piece_label(query_places, starts_ref)
    key_labels = piece_label(key_places, starts_ref)
    return (key_places <= query_places) | (
        (query_labels == key_labels) & (query_labels > 0)
    )


def straddles(starts_ref, edge):
    hit = jnp.int32(0)
    for j in range(starts_ref.shape[0]):
        begin = starts_ref[j]
        hit = jnp.where((begin < edge) & (begin + PIECE > edge), 1, hit)
    return hit


def prep_kernel(pre_ref, square_ref, gain_ref, cos_ref, sin_ref, q_ref, k_ref, v_ref):
    rows = pre_ref.shape[0]
    width = q_ref.shape[1]
    cosine, sine = cos_ref[...], sin_ref[...]
    for which, out_ref in ((0, q_ref), (1, k_ref)):
        square = jnp.broadcast_to(square_ref[which : which + 1, :], (HEAD_DIM, rows)).T
        factor = lax.rsqrt(square * (1.0 / (HEADS * HEAD_DIM)) + norm_epsilon)
        for at in range(0, width, HEAD_DIM):
            low, high = which * width + at, which * width + at + HEAD_DIM
            x = pre_ref[:, low:high] * factor * gain_ref[:, low:high]
            x = x * cosine + pltpu.roll(x, HEAD_DIM // 2, 1) * sine
            out_ref[:, at : at + HEAD_DIM] = x.astype(bf16)
    v_ref[...] = pre_ref[:, 2 * width :].astype(bf16)


def prep(pre, square, gains, cosine, sine):
    rows, triple = pre.shape
    width = triple // 3
    step = 512
    return pl.pallas_call(
        prep_kernel,
        grid=(rows // step,),
        in_specs=[
            pl.BlockSpec((step, triple), lambda i: (i, 0)),
            pl.BlockSpec((2, step), lambda i: (0, i)),
            pl.BlockSpec((1, 2 * width), lambda i: (0, 0)),
            pl.BlockSpec((step, HEAD_DIM), lambda i: (i, 0)),
            pl.BlockSpec((step, HEAD_DIM), lambda i: (i, 0)),
        ],
        out_specs=[pl.BlockSpec((step, width), lambda i: (i, 0))] * 3,
        out_shape=[jax.ShapeDtypeStruct((rows, width), bf16)] * 3,
        cost_estimate=pl.CostEstimate(
            flops=rows * triple * 8, bytes_accessed=rows * triple * 6, transcendentals=0
        ),
        name="prep",
    )(pre, square, gains, cosine, sine)


def attend_kernel(starts_ref, q_ref, k_ref, v_ref, low_ref, mixed_ref, total_ref):
    at = pl.program_id(1)
    query = q_ref[...]
    rows = query.shape[0]

    def step(carry, key_start, key_count, masked):
        row_max, row_sum, mixed = carry
        key = k_ref[pl.ds(key_start, key_count), :]
        value = v_ref[pl.ds(key_start, key_count), :]
        scores = against(query, key) * score_factor
        if masked:
            allowed = allowed_block(starts_ref, at * rows, rows, key_start, key_count)
            scores = jnp.where(allowed, scores, masked_score)
        new_max = jnp.maximum(row_max, jnp.max(scores, axis=1, keepdims=True))
        fade = jnp.exp(row_max - new_max)
        exponent = jnp.exp(scores - new_max)
        row_sum = row_sum * fade + jnp.sum(exponent, axis=1, keepdims=True)
        mixed = mixed * fade + matmul(exponent.astype(bf16), value)
        return new_max, row_sum, mixed

    carry = (
        jnp.full((rows, 1), masked_score, f32),
        jnp.zeros((rows, 1), f32),
        jnp.zeros((rows, HEAD_DIM), f32),
    )
    carry = step(carry, pl.multiple_of(at * rows, rows), rows, True)
    carry = lax.fori_loop(
        0,
        at,
        lambda j, c: step(c, pl.multiple_of(j * rows, rows), rows, False),
        carry,
    )
    edge = (at + 1) * rows
    carry = lax.fori_loop(
        0,
        straddles(starts_ref, edge),
        lambda j, c: step(c, pl.multiple_of(edge, rows), PIECE, True),
        carry,
    )
    row_max, row_sum, mixed = carry
    mixed = mixed / row_sum
    low_ref[...] = mixed.astype(bf16)
    mixed_ref[...] = mixed
    total_ref[...] = jnp.broadcast_to(row_max + jnp.log(row_sum), (rows, HEAD_DIM))


def attend(starts, query, key, value):
    rows, width = query.shape
    heads = width // HEAD_DIM
    block = pl.BlockSpec((BLOCK, HEAD_DIM), lambda h, i, s: (i, h))
    column = pl.BlockSpec((rows, HEAD_DIM), lambda h, i, s: (0, h))
    return pl.pallas_call(
        attend_kernel,
        grid_spec=pltpu.PrefetchScalarGridSpec(
            num_scalar_prefetch=1,
            grid=(heads, rows // BLOCK),
            in_specs=[block, column, column],
            out_specs=[block, block, block],
        ),
        out_shape=[
            jax.ShapeDtypeStruct((rows, width), bf16),
            jax.ShapeDtypeStruct((rows, width), f32),
            jax.ShapeDtypeStruct((rows, width), f32),
        ],
        cost_estimate=pl.CostEstimate(
            flops=heads * rows * rows * HEAD_DIM * 2,
            bytes_accessed=rows * width * 16,
            transcendentals=heads * rows * rows // 2,
        ),
        name="attend",
    )(starts, query, key, value)


def attend_back_kernel(
    starts_ref,
    q_ref,
    grad_ref,
    mixed_ref,
    total_ref,
    k_ref,
    v_ref,
    cos_ref,
    sin_ref,
    dq_ref,
    dk_ref,
    dv_ref,
    dv_total,
):
    at = pl.program_id(1)
    query = q_ref[...]
    grad = grad_ref[...]
    rows = query.shape[0]
    total = total_ref[:, 0:1]
    inner = jnp.sum(grad.astype(f32) * mixed_ref[...], axis=1, keepdims=True)

    @pl.when(at == 0)
    def _():
        dk_ref[...] = jnp.zeros_like(dk_ref)
        dv_total[...] = jnp.zeros_like(dv_total)

    def step(dq, key_start, key_count, masked):
        here = pl.ds(key_start, key_count)
        key = k_ref[here, :]
        value = v_ref[here, :]
        scores = against(query, key) * score_factor
        if masked:
            allowed = allowed_block(starts_ref, at * rows, rows, key_start, key_count)
            scores = jnp.where(allowed, scores, masked_score)
        shares = jnp.exp(scores - total)
        share_grad = against(grad, value)
        score_grad = (shares * (share_grad - inner)).astype(bf16)
        dk_ref[here, :] += across(score_grad, query)
        dv_total[here, :] += across(shares.astype(bf16), grad)
        return dq + matmul(score_grad, key)

    dq = jnp.zeros((rows, HEAD_DIM), f32)
    dq = step(dq, pl.multiple_of(at * rows, rows), rows, True)
    dq = lax.fori_loop(
        0, at, lambda j, c: step(c, pl.multiple_of(j * rows, rows), rows, False), dq
    )
    edge = (at + 1) * rows
    dq = lax.fori_loop(
        0,
        straddles(starts_ref, edge),
        lambda j, c: step(c, pl.multiple_of(edge, rows), PIECE, True),
        dq,
    )

    def unrotated(x, cosine, sine):
        x = x * score_factor
        return x * cosine - pltpu.roll(x, HEAD_DIM // 2, 1) * sine

    mine = pl.ds(pl.multiple_of(at * rows, rows), rows)
    dq_ref[...] = unrotated(dq, cos_ref[mine, :], sin_ref[mine, :])

    @pl.when(at == pl.num_programs(1) - 1)
    def _():
        dk_ref[...] = unrotated(dk_ref[...], cos_ref[...], sin_ref[...])
        dv_ref[...] = dv_total[...].astype(bf16)


def attend_back(starts, query, grad, mixed, total, key, value, cosine, sine):
    rows, width = query.shape
    heads = width // HEAD_DIM
    block = pl.BlockSpec((BLOCK, HEAD_DIM), lambda h, i, s: (i, h))
    column = pl.BlockSpec((rows, HEAD_DIM), lambda h, i, s: (0, h))
    table = pl.BlockSpec((rows, HEAD_DIM), lambda h, i, s: (0, 0))
    return pl.pallas_call(
        attend_back_kernel,
        grid_spec=pltpu.PrefetchScalarGridSpec(
            num_scalar_prefetch=1,
            grid=(heads, rows // BLOCK),
            in_specs=[block, block, block, block, column, column, table, table],
            out_specs=[block, column, column],
            scratch_shapes=[pltpu.VMEM((rows, HEAD_DIM), f32)],
        ),
        out_shape=[
            jax.ShapeDtypeStruct((rows, width), f32),
            jax.ShapeDtypeStruct((rows, width), f32),
            jax.ShapeDtypeStruct((rows, width), bf16),
        ],
        cost_estimate=pl.CostEstimate(
            flops=heads * rows * rows * HEAD_DIM * 5,
            bytes_accessed=rows * width * 28,
            transcendentals=heads * rows * rows // 2,
        ),
        name="attend_back",
    )(starts, query, grad, mixed, total, key, value, cosine, sine)


def body(
    tokens,
    query_weight,
    key_weight,
    value_weight,
    query_norm,
    key_norm,
    output_weight,
    mixer_norm,
    gate_weight,
    up_weight,
    down_weight,
    feeder_norm,
    piece_starts,
    cotangent,
):
    own_rows, model_width = tokens.shape
    group = lax.axis_size("fsdp")
    me = lax.axis_index("fsdp")
    chain = SEQ // own_rows
    spot = me % chain
    width = model_width // chain
    shard = model_width // group
    sequence = ((lax.axis_index("rep") * group + me) * own_rows) // SEQ
    starts = lax.dynamic_index_in_dim(piece_starts, sequence, 0, keepdims=False)
    teams = None
    if group != chain:
        teams = [[b * chain + i for i in range(chain)] for b in range(group // chain)]

    def of_sequence(block):
        return lax.all_gather(block, "fsdp", axis=0, tiled=True, axis_index_groups=teams)

    def to_sequence_rows(block):
        return lax.psum_scatter(
            block.astype(bf16),
            "fsdp",
            scatter_dimension=0,
            tiled=True,
            axis_index_groups=teams,
        ).astype(f32)

    def of_group(block):
        return lax.all_gather(block, "fsdp", axis=0, tiled=True)

    def to_group_rows(block):
        return lax.psum_scatter(
            block.astype(bf16), "fsdp", scatter_dimension=0, tiled=True
        ).astype(f32)

    def placed(block, start, length, axis):
        shape = list(block.shape)
        shape[axis] = length
        return lax.dynamic_update_slice_in_dim(
            jnp.zeros(shape, block.dtype), block, start, axis
        )

    half = HEAD_DIM // 2
    frequency = rope_base ** (-(jnp.arange(half, dtype=f32) * (2.0 / HEAD_DIM)))
    angles = jnp.arange(SEQ, dtype=jnp.int32).astype(f32)[:, None] * frequency[None, :]
    cosine, sine = jnp.cos(angles), jnp.sin(angles)
    cosine = jnp.concatenate([cosine, cosine], axis=1)
    sine = jnp.concatenate([-sine, sine], axis=1)

    own_gains = jnp.stack([query_norm, key_norm, mixer_norm, feeder_norm]).astype(f32)
    gains = xor_sum(placed(own_gains, me * shard, model_width, 1), "fsdp", group)
    pair_gains = lax.dynamic_slice_in_dim(gains[:2], spot * width, width, 1)
    mixer_gain = gains[2:3]
    feeder_gain = gains[3:4]

    rows_weight = jnp.stack([query_weight, key_weight, value_weight], axis=1)
    rows_weight = rows_weight.reshape(shard, 3, chain, width).transpose(2, 0, 1, 3)
    rows_weight = rows_weight.reshape(chain, shard, 3 * width)
    if group != chain:
        rows_weight = jnp.tile(rows_weight, (group // chain, 1, 1))
    triple_weight = lax.all_to_all(rows_weight, "fsdp", 0, 0).reshape(
        model_width, 3 * width
    )
    if group == chain:
        head_output = output_weight
    else:
        head_output = lax.dynamic_slice_in_dim(
            lax.all_gather(output_weight, "fsdp", axis=0, tiled=True),
            spot * width,
            width,
            0,
        )

    all_tokens = of_sequence(tokens)
    pre = matmul(all_tokens, triple_weight)
    query_pre, key_pre = pre[:, :width], pre[:, width : 2 * width]
    squares = jnp.stack(
        [jnp.sum(query_pre * query_pre, axis=1), jnp.sum(key_pre * key_pre, axis=1)]
    )
    squares = xor_sum(squares, "fsdp", chain)
    query_low, key_low, value_low = prep(
        pre, squares, pair_gains.reshape(1, 2 * width), cosine, sine
    )
    mixed_low, mixed, log_total = attend(starts, query_low, key_low, value_low)
    branch_pre = to_sequence_rows(matmul(mixed_low, head_output))
    branch_factor = inverse_rms(branch_pre)
    hidden = tokens.astype(f32) + branch_pre * branch_factor * mixer_gain

    all_hidden = of_group(hidden.astype(bf16))
    gate = matmul(all_hidden, gate_weight).astype(bf16)
    up = matmul(all_hidden, up_weight).astype(bf16)
    gate_wide, up_wide = gate.astype(f32), up.astype(f32)
    sigmoid = jax.nn.sigmoid(gate_wide)
    inner = (gate_wide * sigmoid * up_wide).astype(bf16)
    down_pre = to_group_rows(against(inner, down_weight))
    down_factor = inverse_rms(down_pre)
    result = (hidden + down_pre * down_factor * feeder_gain).astype(bf16)

    tangent = cotangent.astype(f32)
    feeder_part = jnp.sum(tangent * down_pre * down_factor, axis=0)
    down_grad = norm_backward(down_pre, down_factor, feeder_gain, tangent).astype(bf16)
    all_down_grad = of_group(down_grad)
    inner_grad = matmul(all_down_grad, down_weight)
    gate_grad = (
        inner_grad * up_wide * sigmoid * (1.0 + gate_wide * (1.0 - sigmoid))
    ).astype(bf16)
    up_grad = (inner_grad * gate_wide * sigmoid).astype(bf16)
    feed_back = to_group_rows(
        against(gate_grad, gate_weight) + against(up_grad, up_weight)
    )
    hidden_grad = tangent + feed_back
    mixer_part = jnp.sum(hidden_grad * branch_pre * branch_factor, axis=0)
    branch_grad = norm_backward(
        branch_pre, branch_factor, mixer_gain, hidden_grad
    ).astype(bf16)
    gradient_down = rep_sum(across(all_down_grad, inner))
    gradient_gate = rep_sum(across(all_hidden, gate_grad))
    gradient_up = rep_sum(across(all_hidden, up_grad))

    all_branch_grad = of_sequence(branch_grad)
    mixed_grad = against(all_branch_grad, head_output).astype(bf16)
    query_turn, key_turn, value_grad = attend_back(
        starts,
        query_low,
        mixed_grad,
        mixed,
        log_total,
        key_low,
        value_low,
        cosine,
        sine,
    )
    query_gain, key_gain = pair_gains[0:1], pair_gains[1:2]
    means = jnp.stack(
        [
            jnp.sum(query_gain * query_turn * query_pre, axis=1),
            jnp.sum(key_gain * key_turn * key_pre, axis=1),
        ]
    )
    means = xor_sum(means, "fsdp", chain) * (1.0 / model_width)
    factors = lax.rsqrt(squares * (1.0 / model_width) + norm_epsilon)

    def pair_back(turn, pre_part, gain, at):
        factor = factors[at][:, None]
        grad = factor * gain * turn - pre_part * factor * factor * factor * means[at][:, None]
        return grad.astype(bf16), jnp.sum(turn * pre_part * factor, axis=0)

    query_grad, query_part = pair_back(query_turn, query_pre, query_gain, 0)
    key_grad, key_part = pair_back(key_turn, key_pre, key_gain, 1)
    triple_grad = jnp.concatenate([query_grad, key_grad, value_grad], axis=1)
    gradient_tokens = (
        hidden_grad + to_sequence_rows(against(triple_grad, triple_weight))
    ).astype(bf16)

    output_part = across(mixed_low, all_branch_grad)
    triple_part = across(all_tokens, triple_grad)
    if group == chain:
        output_rows = output_part
        triple_rows = lax.all_to_all(
            triple_part.astype(bf16).reshape(chain, shard, 3 * width), "fsdp", 0, 0
        )
        triple_rows = triple_rows.reshape(chain, shard, 3, width).transpose(2, 1, 0, 3)
    else:
        output_rows = to_group_rows(placed(output_part, spot * width, model_width, 0))
        triple_rows = to_group_rows(
            placed(
                triple_part.reshape(model_width, 3, 1, width), spot, chain, 2
            ).reshape(model_width, 3 * model_width)
        )
        triple_rows = triple_rows.reshape(shard, 3, chain, width).transpose(1, 0, 2, 3)
    triple_rows = triple_rows.reshape(3 * shard, model_width)
    triple_rows = jnp.concatenate([triple_rows.astype(bf16), output_rows.astype(bf16)])
    four = rep_sum(triple_rows)

    gain_parts = jnp.stack(
        [
            lax.dynamic_update_slice_in_dim(
                jnp.zeros((model_width,), f32), query_part, spot * width, 0
            ),
            lax.dynamic_update_slice_in_dim(
                jnp.zeros((model_width,), f32), key_part, spot * width, 0
            ),
            mixer_part,
            feeder_part,
        ]
    )
    gain_parts = xor_sum(xor_sum(gain_parts, "fsdp", group), "rep", lax.axis_size("rep"))
    gain_own = lax.dynamic_slice_in_dim(gain_parts, me * shard, shard, 1)
    return (
        result,
        gradient_tokens,
        four[:shard],
        four[shard : 2 * shard],
        four[2 * shard : 3 * shard],
        gain_own[0],
        gain_own[1],
        four[3 * shard :],
        gain_own[2],
        gradient_gate,
        gradient_up,
        gradient_down,
        gain_own[3],
    )


def solution(mesh):
    rows, ends = P(("rep", "fsdp"), None), P(None, "fsdp")
    tops, line = P("fsdp", None), P("fsdp")
    return jax.shard_map(
        body,
        mesh=mesh,
        in_specs=(
            rows, tops, tops, tops, line, line, tops, line, ends, ends, ends, line, P(), rows,
        ),
        out_specs=(
            rows, rows, tops, tops, tops, line, line, tops, line, ends, ends, ends, line,
        ),
        check_vma=False,
    )
```

```python
import jax
import jax.numpy as jnp
from jax import lax
from jax.experimental import pallas as pl
from jax.experimental.pallas import tpu as pltpu
from jax.sharding import PartitionSpec as P

HEADS = 16
HEAD_DIM = 128
SEQ = 2048
PIECE = 256
BLOCK = 512

norm_epsilon = 1e-06
rope_base = 500000.0
masked_score = -1e30
score_factor = HEAD_DIM ** (-0.5)
f32 = jnp.float32
bf16 = jnp.bfloat16


def matmul(a, b):
    return jnp.dot(a, b, preferred_element_type=f32)


def against(a, b):
    return lax.dot_general(a, b, (((1,), (1,)), ((), ())), preferred_element_type=f32)


def across(a, b):
    return lax.dot_general(a, b, (((0,), (0,)), ((), ())), preferred_element_type=f32)


def inverse_rms(values):
    return lax.rsqrt(jnp.mean(values * values, axis=-1, keepdims=True) + norm_epsilon)


def norm_backward(values, factor, gain_row, upstream):
    weighted = upstream * gain_row
    inner_mean = jnp.mean(weighted * values, axis=-1, keepdims=True)
    return factor * weighted - values * (factor * factor * factor) * inner_mean


def swapped(block, axis, bit):
    size = lax.axis_size(axis)
    return lax.ppermute(block, axis, [(i, i ^ bit) for i in range(size)])


def after(block, *others):
    return lax.optimization_barrier((block,) + others)[0]


def xor_sum(block, axis, size):
    bit = 1
    while bit < size:
        block = block + swapped(block, axis, bit)
        bit *= 2
    return block


def replica_bits():
    me = lax.axis_index("rep")
    return (me & 1) == 1, (me & 2) == 2


def shared(piece):
    far = swapped(piece, "rep", 2)
    near = swapped(piece, "rep", 1)
    return [piece, near, far, swapped(far, "rep", 1)]


def in_order(slots):
    odd, high = replica_bits()
    paired = [jnp.where(odd, slots[v ^ 1], slots[v]) for v in range(4)]
    return [jnp.where(high, paired[q ^ 2], paired[q]) for q in range(4)]


def own_part(block, count, which, axis):
    size = block.shape[axis] // count
    start = (lax.axis_index("rep") ^ which) * size
    return lax.dynamic_slice_in_dim(block, start, size, axis)


def piece_label(places, starts_ref):
    label = jnp.where((places >= starts_ref[0]) & (places < starts_ref[0] + PIECE), 1, 0)
    for j in range(1, starts_ref.shape[0]):
        inside = (places >= starts_ref[j]) & (places < starts_ref[j] + PIECE)
        label = jnp.where(inside, j + 1, label)
    return label


def allowed_block(starts_ref, query_start, query_count, key_start, key_count):
    query_places = query_start + lax.broadcasted_iota(jnp.int32, (query_count, 1), 0)
    key_places = key_start + lax.broadcasted_iota(jnp.int32, (1, key_count), 1)
    query_labels = piece_label(query_places, starts_ref)
    key_labels = piece_label(key_places, starts_ref)
    return (key_places <= query_places) | (
        (query_labels == key_labels) & (query_labels > 0)
    )


def straddles(starts_ref, edge):
    hit = jnp.int32(0)
    for j in range(starts_ref.shape[0]):
        begin = starts_ref[j]
        hit = jnp.where((begin < edge) & (begin + PIECE > edge), 1, hit)
    return hit


def prep_kernel(pre_ref, square_ref, gain_ref, cos_ref, sin_ref, q_ref, k_ref, v_ref):
    rows = pre_ref.shape[0]
    width = q_ref.shape[1]
    cosine, sine = cos_ref[...], sin_ref[...]
    for which, out_ref in ((0, q_ref), (1, k_ref)):
        square = jnp.broadcast_to(square_ref[which : which + 1, :], (HEAD_DIM, rows)).T
        factor = lax.rsqrt(square * (1.0 / (HEADS * HEAD_DIM)) + norm_epsilon)
        for at in range(0, width, HEAD_DIM):
            low, high = which * width + at, which * width + at + HEAD_DIM
            x = pre_ref[:, low:high] * factor * gain_ref[:, low:high]
            x = x * cosine + pltpu.roll(x, HEAD_DIM // 2, 1) * sine
            out_ref[:, at : at + HEAD_DIM] = x.astype(bf16)
    v_ref[...] = pre_ref[:, 2 * width :].astype(bf16)


def prep(pre, square, gains, cosine, sine):
    rows, triple = pre.shape
    width = triple // 3
    step = 512
    return pl.pallas_call(
        prep_kernel,
        grid=(rows // step,),
        in_specs=[
            pl.BlockSpec((step, triple), lambda i: (i, 0)),
            pl.BlockSpec((2, step), lambda i: (0, i)),
            pl.BlockSpec((1, 2 * width), lambda i: (0, 0)),
            pl.BlockSpec((step, HEAD_DIM), lambda i: (i, 0)),
            pl.BlockSpec((step, HEAD_DIM), lambda i: (i, 0)),
        ],
        out_specs=[pl.BlockSpec((step, width), lambda i: (i, 0))] * 3,
        out_shape=[jax.ShapeDtypeStruct((rows, width), bf16)] * 3,
        cost_estimate=pl.CostEstimate(
            flops=rows * triple * 8, bytes_accessed=rows * triple * 6, transcendentals=0
        ),
        name="prep",
    )(pre, square, gains, cosine, sine)


def attend_kernel(starts_ref, q_ref, k_ref, v_ref, low_ref, mixed_ref, total_ref):
    at = pl.program_id(1)
    query = q_ref[...]
    rows = query.shape[0]

    def step(carry, key_start, key_count, masked):
        row_max, row_sum, mixed = carry
        key = k_ref[pl.ds(key_start, key_count), :]
        value = v_ref[pl.ds(key_start, key_count), :]
        scores = against(query, key) * score_factor
        if masked:
            allowed = allowed_block(starts_ref, at * rows, rows, key_start, key_count)
            scores = jnp.where(allowed, scores, masked_score)
        new_max = jnp.maximum(row_max, jnp.max(scores, axis=1, keepdims=True))
        fade = jnp.exp(row_max - new_max)
        exponent = jnp.exp(scores - new_max)
        row_sum = row_sum * fade + jnp.sum(exponent, axis=1, keepdims=True)
        mixed = mixed * fade + matmul(exponent.astype(bf16), value)
        return new_max, row_sum, mixed

    carry = (
        jnp.full((rows, 1), masked_score, f32),
        jnp.zeros((rows, 1), f32),
        jnp.zeros((rows, HEAD_DIM), f32),
    )
    carry = step(carry, pl.multiple_of(at * rows, rows), rows, True)
    carry = lax.fori_loop(
        0,
        at,
        lambda j, c: step(c, pl.multiple_of(j * rows, rows), rows, False),
        carry,
    )
    edge = (at + 1) * rows
    carry = lax.fori_loop(
        0,
        straddles(starts_ref, edge),
        lambda j, c: step(c, pl.multiple_of(edge, rows), PIECE, True),
        carry,
    )
    row_max, row_sum, mixed = carry
    mixed = mixed / row_sum
    low_ref[...] = mixed.astype(bf16)
    mixed_ref[...] = mixed
    total_ref[...] = jnp.broadcast_to(row_max + jnp.log(row_sum), (rows, HEAD_DIM))


def attend(starts, query, key, value):
    rows, width = query.shape
    heads = width // HEAD_DIM
    block = pl.BlockSpec((BLOCK, HEAD_DIM), lambda h, i, s: (i, h))
    column = pl.BlockSpec((rows, HEAD_DIM), lambda h, i, s: (0, h))
    return pl.pallas_call(
        attend_kernel,
        grid_spec=pltpu.PrefetchScalarGridSpec(
            num_scalar_prefetch=1,
            grid=(heads, rows // BLOCK),
            in_specs=[block, column, column],
            out_specs=[block, block, block],
        ),
        out_shape=[
            jax.ShapeDtypeStruct((rows, width), bf16),
            jax.ShapeDtypeStruct((rows, width), f32),
            jax.ShapeDtypeStruct((rows, width), f32),
        ],
        cost_estimate=pl.CostEstimate(
            flops=heads * rows * rows * HEAD_DIM * 2,
            bytes_accessed=rows * width * 16,
            transcendentals=heads * rows * rows // 2,
        ),
        name="attend",
    )(starts, query, key, value)


def attend_back_kernel(
    starts_ref,
    q_ref,
    grad_ref,
    mixed_ref,
    total_ref,
    k_ref,
    v_ref,
    cos_ref,
    sin_ref,
    dq_ref,
    dk_ref,
    dv_ref,
    dv_total,
):
    at = pl.program_id(1)
    query = q_ref[...]
    grad = grad_ref[...]
    rows = query.shape[0]
    total = total_ref[:, 0:1]
    inner = jnp.sum(grad.astype(f32) * mixed_ref[...], axis=1, keepdims=True)

    @pl.when(at == 0)
    def _():
        dk_ref[...] = jnp.zeros_like(dk_ref)
        dv_total[...] = jnp.zeros_like(dv_total)

    def step(dq, key_start, key_count, masked):
        here = pl.ds(key_start, key_count)
        key = k_ref[here, :]
        value = v_ref[here, :]
        scores = against(query, key) * score_factor
        if masked:
            allowed = allowed_block(starts_ref, at * rows, rows, key_start, key_count)
            scores = jnp.where(allowed, scores, masked_score)
        shares = jnp.exp(scores - total)
        share_grad = against(grad, value)
        score_grad = (shares * (share_grad - inner)).astype(bf16)
        dk_ref[here, :] += across(score_grad, query)
        dv_total[here, :] += across(shares.astype(bf16), grad)
        return dq + matmul(score_grad, key)

    dq = jnp.zeros((rows, HEAD_DIM), f32)
    dq = step(dq, pl.multiple_of(at * rows, rows), rows, True)
    dq = lax.fori_loop(
        0, at, lambda j, c: step(c, pl.multiple_of(j * rows, rows), rows, False), dq
    )
    edge = (at + 1) * rows
    dq = lax.fori_loop(
        0,
        straddles(starts_ref, edge),
        lambda j, c: step(c, pl.multiple_of(edge, rows), PIECE, True),
        dq,
    )

    def unrotated(x, cosine, sine):
        x = x * score_factor
        return x * cosine - pltpu.roll(x, HEAD_DIM // 2, 1) * sine

    mine = pl.ds(pl.multiple_of(at * rows, rows), rows)
    dq_ref[...] = unrotated(dq, cos_ref[mine, :], sin_ref[mine, :])

    @pl.when(at == pl.num_programs(1) - 1)
    def _():
        dk_ref[...] = unrotated(dk_ref[...], cos_ref[...], sin_ref[...])
        dv_ref[...] = dv_total[...].astype(bf16)


def attend_back(starts, query, grad, mixed, total, key, value, cosine, sine):
    rows, width = query.shape
    heads = width // HEAD_DIM
    block = pl.BlockSpec((BLOCK, HEAD_DIM), lambda h, i, s: (i, h))
    column = pl.BlockSpec((rows, HEAD_DIM), lambda h, i, s: (0, h))
    table = pl.BlockSpec((rows, HEAD_DIM), lambda h, i, s: (0, 0))
    return pl.pallas_call(
        attend_back_kernel,
        grid_spec=pltpu.PrefetchScalarGridSpec(
            num_scalar_prefetch=1,
            grid=(heads, rows // BLOCK),
            in_specs=[block, block, block, block, column, column, table, table],
            out_specs=[block, column, column],
            scratch_shapes=[pltpu.VMEM((rows, HEAD_DIM), f32)],
        ),
        out_shape=[
            jax.ShapeDtypeStruct((rows, width), f32),
            jax.ShapeDtypeStruct((rows, width), f32),
            jax.ShapeDtypeStruct((rows, width), bf16),
        ],
        cost_estimate=pl.CostEstimate(
            flops=heads * rows * rows * HEAD_DIM * 5,
            bytes_accessed=rows * width * 28,
            transcendentals=heads * rows * rows // 2,
        ),
        name="attend_back",
    )(starts, query, grad, mixed, total, key, value, cosine, sine)


def body(
    tokens,
    query_weight,
    key_weight,
    value_weight,
    query_norm,
    key_norm,
    output_weight,
    mixer_norm,
    gate_weight,
    up_weight,
    down_weight,
    feeder_norm,
    piece_starts,
    cotangent,
):
    own_rows, model_width = tokens.shape
    group = lax.axis_size("fsdp")
    assert lax.axis_size("rep") == 4 and group % 4 == 0
    me = lax.axis_index("fsdp")
    chain = SEQ // own_rows
    spot = me % chain
    width = model_width // chain
    shard = model_width // group
    part = shard // 4
    sequence = ((lax.axis_index("rep") * group + me) * own_rows) // SEQ
    starts = lax.dynamic_index_in_dim(piece_starts, sequence, 0, keepdims=False)
    teams = None
    if group != chain:
        teams = [[b * chain + i for i in range(chain)] for b in range(group // chain)]
    strides = [[r + 4 * m for m in range(group // 4)] for r in range(4)]

    def of_sequence(block):
        return lax.all_gather(block, "fsdp", axis=0, tiled=True, axis_index_groups=teams)

    def to_sequence_rows(block):
        return lax.psum_scatter(
            block.astype(bf16),
            "fsdp",
            scatter_dimension=0,
            tiled=True,
            axis_index_groups=teams,
        ).astype(f32)

    def to_group_rows(block):
        return lax.psum_scatter(
            block.astype(bf16), "fsdp", scatter_dimension=0, tiled=True
        ).astype(f32)

    def exchanged(block):
        return lax.all_to_all(block, "fsdp", 0, 0, axis_index_groups=teams)

    def of_quad(block):
        half = block.shape[0] // 2
        along_y = swapped(block, "fsdp", 1)
        along_z = swapped(block, "fsdp", 2)
        top = swapped(along_y[:half], "fsdp", 2)
        bottom = swapped(along_z[half:], "fsdp", 1)
        return jnp.concatenate([block, along_y, along_z, top, bottom])

    def to_quad_rows(terms, fill=None):
        half = own_rows // 2
        across_rows = terms(3 * own_rows, 4 * own_rows).astype(bf16)
        top = swapped(across_rows[:half], "fsdp", 2)
        bottom = swapped(across_rows[half:], "fsdp", 1)
        middle = terms(own_rows, 3 * own_rows)
        y_rows = jnp.concatenate(
            [middle[:half] + top.astype(f32), middle[half:own_rows]]
        ).astype(bf16)
        z_rows = jnp.concatenate(
            [
                middle[own_rows : own_rows + half],
                middle[own_rows + half :] + bottom.astype(f32),
            ]
        ).astype(bf16)
        from_y = swapped(y_rows, "fsdp", 1)
        from_z = swapped(z_rows, "fsdp", 2)
        own = terms(0, own_rows, y_rows, z_rows)
        if fill is not None:
            from_y = after(from_y, *fill(own))
        return own + from_y.astype(f32) + from_z.astype(f32)

    def widened(weight, first, second):
        if group != 8:
            return lax.all_gather(
                weight, "fsdp", axis=1, tiled=True, axis_index_groups=strides
            )
        theirs = swapped(after(own_part(weight, 4, 0, 1), first), "fsdp", 4)
        theirs = shared(after(theirs, second))
        blocks = []
        for v in (0, 2, 1, 3):
            blocks += [own_part(weight, 4, v, 1), theirs[v]]
        return jnp.concatenate(blocks, axis=1)

    def replica_columns(pieces):
        size = pieces[0].shape[1]
        whole = jnp.zeros((pieces[0].shape[0], 4 * size), f32)
        for v, block in enumerate(pieces):
            start = (lax.axis_index("rep") ^ v) * size
            whole = lax.dynamic_update_slice_in_dim(whole, block.astype(f32), start, 1)
        return whole

    def send_terms(rows, units):
        return across(rows, units[:, units.shape[1] // 2 :]).astype(bf16)

    def keep_terms(rows, units, near):
        total = across(rows, units[:, : units.shape[1] // 2]) + near.astype(f32)
        half = total.shape[1] // 2
        return total[:, :half], total[:, half:].astype(bf16)

    def to_partner(kept, far):
        total = kept + far.astype(f32)
        half = total.shape[1] // 2
        return total[:, :half], total[:, half:].astype(bf16)

    def narrowed_whole(rows, units):
        total = lax.psum_scatter(
            across(rows, units).astype(bf16),
            "fsdp",
            scatter_dimension=1,
            tiled=True,
            axis_index_groups=strides,
        )
        return lax.psum(total, "rep").astype(f32)

    half = HEAD_DIM // 2
    frequency = rope_base ** (-(jnp.arange(half, dtype=f32) * (2.0 / HEAD_DIM)))
    angles = jnp.arange(SEQ, dtype=jnp.int32).astype(f32)[:, None] * frequency[None, :]
    cosine, sine = jnp.cos(angles), jnp.sin(angles)
    cosine = jnp.concatenate([cosine, cosine], axis=1)
    sine = jnp.concatenate([-sine, sine], axis=1)

    rows_weight = jnp.stack(
        [own_part(w, 4, 0, 0) for w in (query_weight, key_weight, value_weight)], axis=1
    )
    rows_weight = rows_weight.reshape(part, 3, chain, width).transpose(2, 0, 1, 3)
    rows_weight = rows_weight.reshape(chain, part, 3 * width)
    if group != chain:
        rows_weight = jnp.tile(rows_weight, (group // chain, 1, 1))
    columns_weight = lax.all_to_all(rows_weight, "fsdp", 0, 0)
    triple_weight = jnp.stack(in_order(shared(columns_weight)), axis=1).reshape(
        model_width, 3 * width
    )
    all_tokens = of_sequence(tokens)

    own_gains = jnp.stack([query_norm, key_norm, mixer_norm, feeder_norm]).astype(f32)
    gains = lax.dynamic_update_slice_in_dim(
        jnp.zeros((4, model_width), f32), own_gains, me * shard, 1
    )
    gains = xor_sum(gains, "fsdp", group)
    if group == chain:
        pair_gains = own_gains[:2]
    else:
        pair_gains = lax.dynamic_slice_in_dim(gains[:2], spot * width, width, 1)
    mixer_gain = gains[2:3]
    feeder_gain = gains[3:4]

    pre = matmul(all_tokens, triple_weight)
    query_pre, key_pre = pre[:, :width], pre[:, width : 2 * width]
    squares = jnp.stack(
        [jnp.sum(query_pre * query_pre, axis=1), jnp.sum(key_pre * key_pre, axis=1)]
    )
    squares = xor_sum(squares, "fsdp", chain)
    query_low, key_low, value_low = prep(
        pre, squares, pair_gains.reshape(1, 2 * width), cosine, sine
    )
    output_piece = lax.all_gather(
        after(own_part(output_weight, 4, 0, 1), all_tokens), "fsdp", axis=0, tiled=True
    )
    output_slots = shared(after(output_piece, query_low))
    whole_output = jnp.concatenate([output_slots[v] for v in (0, 2, 1, 3)], axis=1)

    mixed_low, mixed, log_total = attend(starts, query_low, key_low, value_low)
    mixed_rows = exchanged(mixed_low.reshape(chain, own_rows, width))
    mixed_rows = mixed_rows.transpose(1, 0, 2).reshape(own_rows, model_width)
    branch_near = matmul(mixed_rows, whole_output)
    quarter = model_width // 4
    branch_slots = [branch_near[:, i * quarter : (i + 1) * quarter] for i in (0, 2, 1, 3)]
    branch_pre = jnp.concatenate(in_order(branch_slots), axis=1)
    branch_factor = inverse_rms(branch_pre)
    hidden = tokens.astype(f32) + branch_pre * branch_factor * mixer_gain

    wide_gate = widened(gate_weight, columns_weight, mixed_low)
    wide_up = widened(up_weight, all_tokens, mixed_rows)
    wide_down = widened(down_weight, query_low, hidden)
    all_hidden = of_quad(hidden.astype(bf16))
    gate = matmul(all_hidden, wide_gate).astype(bf16)
    up = matmul(all_hidden, wide_up).astype(bf16)
    gate_wide, up_wide = gate.astype(f32), up.astype(f32)
    sigmoid = jax.nn.sigmoid(gate_wide)
    inner = (gate_wide * sigmoid * up_wide).astype(bf16)
    def down_terms(low, high, *deps):
        return against(after(inner[low:high], *deps), wide_down)

    down_pre = to_quad_rows(down_terms)
    down_factor = inverse_rms(down_pre)
    result = (hidden + down_pre * down_factor * feeder_gain).astype(bf16)

    tangent = cotangent.astype(f32)
    feeder_part = jnp.sum(tangent * down_pre * down_factor, axis=0)
    down_grad = norm_backward(down_pre, down_factor, feeder_gain, tangent).astype(bf16)
    all_down_grad = of_quad(down_grad)
    inner_grad = matmul(all_down_grad, wide_down)
    gate_grad = (
        inner_grad * up_wide * sigmoid * (1.0 + gate_wide * (1.0 - sigmoid))
    ).astype(bf16)
    up_grad = (inner_grad * gate_wide * sigmoid).astype(bf16)
    stage = {}

    def early_gradients(own):
        if group != 8:
            return ()
        down_send = send_terms(all_down_grad, after(inner, own))
        down_near = swapped(down_send, "rep", 1)
        gate_send = send_terms(all_hidden, after(gate_grad, down_send))
        stage["gate_near"] = swapped(gate_send, "rep", 1)
        stage["down_kept"], down_pass = keep_terms(
            all_down_grad, after(inner, gate_send), down_near
        )
        stage["down_far"] = swapped(down_pass, "rep", 2)
        return (down_pass,)

    def back_terms(low, high, *deps):
        return against(after(gate_grad[low:high], *deps), wide_gate) + against(
            after(up_grad[low:high], *deps), wide_up
        )

    feed_back = to_quad_rows(back_terms, early_gradients)
    hidden_grad = tangent + feed_back
    mixer_part = jnp.sum(hidden_grad * branch_pre * branch_factor, axis=0)
    branch_grad = norm_backward(
        branch_pre, branch_factor, mixer_gain, hidden_grad
    ).astype(bf16)

    grad_near = jnp.concatenate(
        [own_part(branch_grad, 4, v, 1) for v in (0, 2, 1, 3)], axis=1
    )
    mixed_grad_rows = against(grad_near, whole_output).astype(bf16)
    mixed_grad = exchanged(
        mixed_grad_rows.reshape(own_rows, chain, width).transpose(1, 0, 2)
    ).reshape(chain * own_rows, width)
    output_half = model_width // 2
    late_rows = after(mixed_rows, mixed_grad_rows)
    output_send = across(late_rows, grad_near[:, output_half:]).astype(bf16)
    output_near = swapped(output_send, "rep", 1)
    if group == 8:
        gate_kept, gate_pass = keep_terms(
            all_hidden, after(gate_grad, output_send), stage["gate_near"]
        )
        late_rows = after(mixed_rows, gate_pass)
    output_kept = across(late_rows, grad_near[:, :output_half]) + output_near.astype(f32)
    output_pass = output_kept[:, quarter:].astype(bf16)
    output_kept = output_kept[:, :quarter]
    output_far = swapped(output_pass, "rep", 2)
    if group == 8:
        gate_far = swapped(after(gate_pass, output_pass), "rep", 2)
        up_send = send_terms(all_hidden, after(up_grad, output_pass))
        up_near = swapped(up_send, "rep", 1)
        mixed_grad = after(mixed_grad, up_send)
    query_turn, key_turn, value_grad = attend_back(
        starts,
        query_low,
        mixed_grad,
        mixed,
        log_total,
        key_low,
        value_low,
        cosine,
        sine,
    )
    query_gain, key_gain = pair_gains[0:1], pair_gains[1:2]
    means = jnp.stack(
        [
            jnp.sum(query_gain * query_turn * query_pre, axis=1),
            jnp.sum(key_gain * key_turn * key_pre, axis=1),
        ]
    )
    if group == 8:
        down_kept, down_pass = to_partner(
            stage["down_kept"], after(stage["down_far"], value_grad)
        )
        down_theirs = swapped(down_pass, "fsdp", 4)
        means = after(means, down_pass)
    means = xor_sum(means, "fsdp", chain) * (1.0 / model_width)
    factors = lax.rsqrt(squares * (1.0 / model_width) + norm_epsilon)

    def pair_back(turn, pre_part, gain, at):
        factor = factors[at][:, None]
        grad = factor * gain * turn - pre_part * factor * factor * factor * means[at][:, None]
        return grad.astype(bf16), jnp.sum(turn * pre_part * factor, axis=0)

    query_grad, query_part = pair_back(query_turn, query_pre, query_gain, 0)
    key_grad, key_part = pair_back(key_turn, key_pre, key_gain, 1)
    triple_grad = jnp.concatenate([query_grad, key_grad, value_grad], axis=1)
    output_part = (output_kept + after(output_far, triple_grad).astype(f32)).astype(bf16)
    token_terms = against(triple_grad, triple_weight).astype(bf16)
    output_part = to_group_rows(output_part)
    token_rows = to_sequence_rows(token_terms)
    gradient_tokens = (hidden_grad + token_rows).astype(bf16)

    triple_part = across(all_tokens, after(triple_grad, token_terms))
    if group == chain:
        triple_part = triple_part.reshape(chain, 4, part, 3 * width)
        slots = [own_part(triple_part, 4, v, 1)[:, 0] for v in range(4)]
        sends = [slots[v].astype(bf16) for v in (3, 1)]
        near = [swapped(x, "rep", 1) for x in sends]
        if group == 8:
            up_kept, up_pass = keep_terms(all_hidden, after(up_grad, *sends), up_near)
            up_far = swapped(up_pass, "rep", 2)
            near = [after(x, up_pass) for x in near]
        passed = (slots[2] + near[0].astype(f32)).astype(bf16)
        kept = slots[0] + near[1].astype(f32)
        passed_far = swapped(passed, "rep", 2)
        if group == 8:
            gate_kept, gate_pass = to_partner(gate_kept, after(gate_far, passed))
            gate_theirs = swapped(gate_pass, "fsdp", 4)
            down_theirs = after(down_theirs, gate_pass)
            down_total = (down_kept + down_theirs.astype(f32)).astype(bf16)
            down_pieces = shared(down_total)
            passed_far = after(passed_far, down_total)
        kept = (kept + passed_far.astype(f32)).astype(bf16)
        heads_rows = lax.all_to_all(kept, "fsdp", 0, 0)
        if group == 8:
            up_kept, up_pass = to_partner(up_kept, after(up_far, kept))
            up_theirs = swapped(up_pass, "fsdp", 4)
            output_part = after(output_part, up_pass)
        output_total = output_part.astype(bf16)
        output_pieces = shared(output_total)
        if group == 8:
            gate_theirs = after(gate_theirs, output_total)
            gate_total = (gate_kept + gate_theirs.astype(f32)).astype(bf16)
            gate_pieces = shared(gate_total)
            heads_rows = after(heads_rows, gate_total)
        triple_pieces = shared(heads_rows)
        if group == 8:
            up_theirs = after(up_theirs, heads_rows)
            up_total = (up_kept + up_theirs.astype(f32)).astype(bf16)
            up_pieces = shared(up_total)
            gradient_down = replica_columns(down_pieces)
            gradient_gate = replica_columns(gate_pieces)
            gradient_up = replica_columns(up_pieces)
        gradient_output = replica_columns(output_pieces)
        triple_rows = jnp.stack(in_order(triple_pieces))
        triple_rows = triple_rows.reshape(4, chain, part, 3, width)
        triple_rows = triple_rows.transpose(3, 0, 2, 1, 4).reshape(3, shard, model_width)
    else:
        gradient_output = replica_columns(shared(output_part.astype(bf16)))
        triple_rows = lax.dynamic_update_slice_in_dim(
            jnp.zeros((model_width, 3, chain, width), f32),
            triple_part.reshape(model_width, 3, 1, width),
            spot,
            2,
        )
        triple_rows = to_group_rows(triple_rows.reshape(model_width, 3 * model_width))
        triple_rows = lax.psum(triple_rows.astype(bf16), "rep")
        triple_rows = triple_rows.reshape(shard, 3, model_width).transpose(1, 0, 2)
    if group != 8:
        gradient_down = narrowed_whole(all_down_grad, inner)
        gradient_gate = narrowed_whole(all_hidden, gate_grad)
        gradient_up = narrowed_whole(all_hidden, up_grad)
    triple_rows = triple_rows.astype(f32)

    gain_parts = jnp.stack(
        [
            lax.dynamic_update_slice_in_dim(
                jnp.zeros((model_width,), f32), query_part, spot * width, 0
            ),
            lax.dynamic_update_slice_in_dim(
                jnp.zeros((model_width,), f32), key_part, spot * width, 0
            ),
            mixer_part,
            feeder_part,
        ]
    )
    gain_parts = xor_sum(xor_sum(gain_parts, "fsdp", group), "rep", 4)
    gain_own = lax.dynamic_slice_in_dim(gain_parts, me * shard, shard, 1)
    return (
        result,
        gradient_tokens,
        triple_rows[0],
        triple_rows[1],
        triple_rows[2],
        gain_own[0],
        gain_own[1],
        gradient_output,
        gain_own[2],
        gradient_gate,
        gradient_up,
        gradient_down,
        gain_own[3],
    )


def solution(mesh):
    rows, ends = P(("rep", "fsdp"), None), P(None, "fsdp")
    tops, line = P("fsdp", None), P("fsdp")
    return jax.shard_map(
        body,
        mesh=mesh,
        in_specs=(
            rows, tops, tops, tops, line, line, tops, line, ends, ends, ends, line, P(), rows,
        ),
        out_specs=(
            rows, rows, tops, tops, tops, line, line, tops, line, ends, ends, ends, line,
        ),
        check_vma=False,
    )
```

```python
import jax
import jax.numpy as jnp
from jax import lax
from jax.experimental import pallas as pl
from jax.experimental.pallas import tpu as pltpu
from jax.sharding import PartitionSpec as P

HEADS = 16
HEAD_DIM = 128
SEQ = 2048
PIECE = 256
BLOCK = 512

norm_epsilon = 1e-06
rope_base = 500000.0
masked_score = -1e30
score_factor = HEAD_DIM ** (-0.5)
f32 = jnp.float32
bf16 = jnp.bfloat16


def matmul(a, b):
    return jnp.dot(a, b, preferred_element_type=f32)


def against(a, b):
    return lax.dot_general(a, b, (((1,), (1,)), ((), ())), preferred_element_type=f32)


def across(a, b):
    return lax.dot_general(a, b, (((0,), (0,)), ((), ())), preferred_element_type=f32)


def inverse_rms(values):
    return lax.rsqrt(jnp.mean(values * values, axis=-1, keepdims=True) + norm_epsilon)


def norm_backward(values, factor, gain_row, upstream):
    weighted = upstream * gain_row
    inner_mean = jnp.mean(weighted * values, axis=-1, keepdims=True)
    return factor * weighted - values * (factor * factor * factor) * inner_mean


def swapped(block, axis, bit):
    size = lax.axis_size(axis)
    return lax.ppermute(block, axis, [(i, i ^ bit) for i in range(size)])


def after(block, *others):
    return lax.optimization_barrier((block,) + others)[0]


def xor_sum(block, axis, size):
    bit = 1
    while bit < size:
        block = block + swapped(block, axis, bit)
        bit *= 2
    return block


def replica_bits():
    me = lax.axis_index("rep")
    return (me & 1) == 1, (me & 2) == 2


def shared(piece):
    far = swapped(piece, "rep", 2)
    near = swapped(piece, "rep", 1)
    return [piece, near, far, swapped(far, "rep", 1)]


def in_order(slots):
    odd, high = replica_bits()
    paired = [jnp.where(odd, slots[v ^ 1], slots[v]) for v in range(4)]
    return [jnp.where(high, paired[q ^ 2], paired[q]) for q in range(4)]


def own_part(block, count, which, axis):
    size = block.shape[axis] // count
    start = (lax.axis_index("rep") ^ which) * size
    return lax.dynamic_slice_in_dim(block, start, size, axis)


def piece_label(places, starts_ref):
    label = jnp.where((places >= starts_ref[0]) & (places < starts_ref[0] + PIECE), 1, 0)
    for j in range(1, starts_ref.shape[0]):
        inside = (places >= starts_ref[j]) & (places < starts_ref[j] + PIECE)
        label = jnp.where(inside, j + 1, label)
    return label


def allowed_block(starts_ref, query_start, query_count, key_start, key_count):
    query_places = query_start + lax.broadcasted_iota(jnp.int32, (query_count, 1), 0)
    key_places = key_start + lax.broadcasted_iota(jnp.int32, (1, key_count), 1)
    query_labels = piece_label(query_places, starts_ref)
    key_labels = piece_label(key_places, starts_ref)
    return (key_places <= query_places) | (
        (query_labels == key_labels) & (query_labels > 0)
    )


def straddles(starts_ref, edge):
    hit = jnp.int32(0)
    for j in range(starts_ref.shape[0]):
        begin = starts_ref[j]
        hit = jnp.where((begin < edge) & (begin + PIECE > edge), 1, hit)
    return hit


def prep_kernel(pre_ref, square_ref, gain_ref, cos_ref, sin_ref, q_ref, k_ref, v_ref):
    rows = pre_ref.shape[0]
    width = q_ref.shape[1]
    cosine, sine = cos_ref[...], sin_ref[...]
    for which, out_ref in ((0, q_ref), (1, k_ref)):
        square = jnp.broadcast_to(square_ref[which : which + 1, :], (HEAD_DIM, rows)).T
        factor = lax.rsqrt(square * (1.0 / (HEADS * HEAD_DIM)) + norm_epsilon)
        for at in range(0, width, HEAD_DIM):
            low, high = which * width + at, which * width + at + HEAD_DIM
            x = pre_ref[:, low:high] * factor * gain_ref[:, low:high]
            x = x * cosine + pltpu.roll(x, HEAD_DIM // 2, 1) * sine
            out_ref[:, at : at + HEAD_DIM] = x.astype(bf16)
    v_ref[...] = pre_ref[:, 2 * width :].astype(bf16)


def prep(pre, square, gains, cosine, sine):
    rows, triple = pre.shape
    width = triple // 3
    step = 512
    return pl.pallas_call(
        prep_kernel,
        grid=(rows // step,),
        in_specs=[
            pl.BlockSpec((step, triple), lambda i: (i, 0)),
            pl.BlockSpec((2, step), lambda i: (0, i)),
            pl.BlockSpec((1, 2 * width), lambda i: (0, 0)),
            pl.BlockSpec((step, HEAD_DIM), lambda i: (i, 0)),
            pl.BlockSpec((step, HEAD_DIM), lambda i: (i, 0)),
        ],
        out_specs=[pl.BlockSpec((step, width), lambda i: (i, 0))] * 3,
        out_shape=[jax.ShapeDtypeStruct((rows, width), bf16)] * 3,
        cost_estimate=pl.CostEstimate(
            flops=rows * triple * 8, bytes_accessed=rows * triple * 6, transcendentals=0
        ),
        name="prep",
    )(pre, square, gains, cosine, sine)


def attend_kernel(starts_ref, q_ref, k_ref, v_ref, low_ref, mixed_ref, total_ref):
    at = pl.program_id(1)
    query = q_ref[...]
    rows = query.shape[0]

    def step(carry, key_start, key_count, masked):
        row_max, row_sum, mixed = carry
        key = k_ref[pl.ds(key_start, key_count), :]
        value = v_ref[pl.ds(key_start, key_count), :]
        scores = against(query, key) * score_factor
        if masked:
            allowed = allowed_block(starts_ref, at * rows, rows, key_start, key_count)
            scores = jnp.where(allowed, scores, masked_score)
        new_max = jnp.maximum(row_max, jnp.max(scores, axis=1, keepdims=True))
        fade = jnp.exp(row_max - new_max)
        exponent = jnp.exp(scores - new_max)
        row_sum = row_sum * fade + jnp.sum(exponent, axis=1, keepdims=True)
        mixed = mixed * fade + matmul(exponent.astype(bf16), value)
        return new_max, row_sum, mixed

    carry = (
        jnp.full((rows, 1), masked_score, f32),
        jnp.zeros((rows, 1), f32),
        jnp.zeros((rows, HEAD_DIM), f32),
    )
    carry = step(carry, pl.multiple_of(at * rows, rows), rows, True)
    carry = lax.fori_loop(
        0,
        at,
        lambda j, c: step(c, pl.multiple_of(j * rows, rows), rows, False),
        carry,
    )
    edge = (at + 1) * rows
    carry = lax.fori_loop(
        0,
        straddles(starts_ref, edge),
        lambda j, c: step(c, pl.multiple_of(edge, rows), PIECE, True),
        carry,
    )
    row_max, row_sum, mixed = carry
    mixed = mixed / row_sum
    low_ref[...] = mixed.astype(bf16)
    mixed_ref[...] = mixed
    total_ref[...] = jnp.broadcast_to(row_max + jnp.log(row_sum), (rows, HEAD_DIM))


def attend(starts, query, key, value):
    rows, width = query.shape
    heads = width // HEAD_DIM
    block = pl.BlockSpec((BLOCK, HEAD_DIM), lambda h, i, s: (i, h))
    column = pl.BlockSpec((rows, HEAD_DIM), lambda h, i, s: (0, h))
    return pl.pallas_call(
        attend_kernel,
        grid_spec=pltpu.PrefetchScalarGridSpec(
            num_scalar_prefetch=1,
            grid=(heads, rows // BLOCK),
            in_specs=[block, column, column],
            out_specs=[block, block, block],
        ),
        out_shape=[
            jax.ShapeDtypeStruct((rows, width), bf16),
            jax.ShapeDtypeStruct((rows, width), f32),
            jax.ShapeDtypeStruct((rows, width), f32),
        ],
        cost_estimate=pl.CostEstimate(
            flops=heads * rows * rows * HEAD_DIM * 2,
            bytes_accessed=rows * width * 16,
            transcendentals=heads * rows * rows // 2,
        ),
        name="attend",
    )(starts, query, key, value)


def attend_back_kernel(
    starts_ref,
    q_ref,
    grad_ref,
    mixed_ref,
    total_ref,
    k_ref,
    v_ref,
    cos_ref,
    sin_ref,
    dq_ref,
    dk_ref,
    dv_ref,
    dv_total,
):
    at = pl.program_id(1)
    query = q_ref[...]
    grad = grad_ref[...]
    rows = query.shape[0]
    total = total_ref[:, 0:1]
    inner = jnp.sum(grad.astype(f32) * mixed_ref[...], axis=1, keepdims=True)

    @pl.when(at == 0)
    def _():
        dk_ref[...] = jnp.zeros_like(dk_ref)
        dv_total[...] = jnp.zeros_like(dv_total)

    def step(dq, key_start, key_count, masked):
        here = pl.ds(key_start, key_count)
        key = k_ref[here, :]
        value = v_ref[here, :]
        scores = against(query, key) * score_factor
        if masked:
            allowed = allowed_block(starts_ref, at * rows, rows, key_start, key_count)
            scores = jnp.where(allowed, scores, masked_score)
        shares = jnp.exp(scores - total)
        share_grad = against(grad, value)
        score_grad = (shares * (share_grad - inner)).astype(bf16)
        dk_ref[here, :] += across(score_grad, query)
        dv_total[here, :] += across(shares.astype(bf16), grad)
        return dq + matmul(score_grad, key)

    dq = jnp.zeros((rows, HEAD_DIM), f32)
    dq = step(dq, pl.multiple_of(at * rows, rows), rows, True)
    dq = lax.fori_loop(
        0, at, lambda j, c: step(c, pl.multiple_of(j * rows, rows), rows, False), dq
    )
    edge = (at + 1) * rows
    dq = lax.fori_loop(
        0,
        straddles(starts_ref, edge),
        lambda j, c: step(c, pl.multiple_of(edge, rows), PIECE, True),
        dq,
    )

    def unrotated(x, cosine, sine):
        x = x * score_factor
        return x * cosine - pltpu.roll(x, HEAD_DIM // 2, 1) * sine

    mine = pl.ds(pl.multiple_of(at * rows, rows), rows)
    dq_ref[...] = unrotated(dq, cos_ref[mine, :], sin_ref[mine, :])

    @pl.when(at == pl.num_programs(1) - 1)
    def _():
        dk_ref[...] = unrotated(dk_ref[...], cos_ref[...], sin_ref[...])
        dv_ref[...] = dv_total[...].astype(bf16)


def attend_back(starts, query, grad, mixed, total, key, value, cosine, sine):
    rows, width = query.shape
    heads = width // HEAD_DIM
    block = pl.BlockSpec((BLOCK, HEAD_DIM), lambda h, i, s: (i, h))
    column = pl.BlockSpec((rows, HEAD_DIM), lambda h, i, s: (0, h))
    table = pl.BlockSpec((rows, HEAD_DIM), lambda h, i, s: (0, 0))
    return pl.pallas_call(
        attend_back_kernel,
        grid_spec=pltpu.PrefetchScalarGridSpec(
            num_scalar_prefetch=1,
            grid=(heads, rows // BLOCK),
            in_specs=[block, block, block, block, column, column, table, table],
            out_specs=[block, column, column],
            scratch_shapes=[pltpu.VMEM((rows, HEAD_DIM), f32)],
        ),
        out_shape=[
            jax.ShapeDtypeStruct((rows, width), f32),
            jax.ShapeDtypeStruct((rows, width), f32),
            jax.ShapeDtypeStruct((rows, width), bf16),
        ],
        cost_estimate=pl.CostEstimate(
            flops=heads * rows * rows * HEAD_DIM * 5,
            bytes_accessed=rows * width * 28,
            transcendentals=heads * rows * rows // 2,
        ),
        name="attend_back",
    )(starts, query, grad, mixed, total, key, value, cosine, sine)


def body(
    tokens,
    query_weight,
    key_weight,
    value_weight,
    query_norm,
    key_norm,
    output_weight,
    mixer_norm,
    gate_weight,
    up_weight,
    down_weight,
    feeder_norm,
    piece_starts,
    cotangent,
):
    own_rows, model_width = tokens.shape
    group = lax.axis_size("fsdp")
    assert lax.axis_size("rep") == 4 and group % 4 == 0
    me = lax.axis_index("fsdp")
    chain = SEQ // own_rows
    spot = me % chain
    width = model_width // chain
    shard = model_width // group
    part = shard // 4
    sequence = ((lax.axis_index("rep") * group + me) * own_rows) // SEQ
    starts = lax.dynamic_index_in_dim(piece_starts, sequence, 0, keepdims=False)
    teams = None
    if group != chain:
        teams = [[b * chain + i for i in range(chain)] for b in range(group // chain)]
    strides = [[r + 4 * m for m in range(group // 4)] for r in range(4)]

    def of_sequence(block):
        return lax.all_gather(block, "fsdp", axis=0, tiled=True, axis_index_groups=teams)

    def to_sequence_rows(block):
        return lax.psum_scatter(
            block.astype(bf16),
            "fsdp",
            scatter_dimension=0,
            tiled=True,
            axis_index_groups=teams,
        ).astype(f32)

    def to_group_rows(block):
        return lax.psum_scatter(
            block.astype(bf16), "fsdp", scatter_dimension=0, tiled=True
        ).astype(f32)

    def exchanged(block):
        return lax.all_to_all(block, "fsdp", 0, 0, axis_index_groups=teams)

    def of_quad(block):
        half = block.shape[0] // 2
        along_y = swapped(block, "fsdp", 1)
        along_z = swapped(block, "fsdp", 2)
        top = swapped(along_y[:half], "fsdp", 2)
        bottom = swapped(along_z[half:], "fsdp", 1)
        return jnp.concatenate([block, along_y, along_z, top, bottom])

    def to_quad_rows(terms, fill=None):
        half = own_rows // 2
        across_rows = terms(3 * own_rows, 4 * own_rows).astype(bf16)
        top = swapped(across_rows[:half], "fsdp", 2)
        bottom = swapped(across_rows[half:], "fsdp", 1)
        middle = terms(own_rows, 3 * own_rows)
        y_rows = jnp.concatenate(
            [middle[:half] + top.astype(f32), middle[half:own_rows]]
        ).astype(bf16)
        z_rows = jnp.concatenate(
            [
                middle[own_rows : own_rows + half],
                middle[own_rows + half :] + bottom.astype(f32),
            ]
        ).astype(bf16)
        from_y = swapped(y_rows, "fsdp", 1)
        from_z = swapped(z_rows, "fsdp", 2)
        own = terms(0, own_rows, y_rows, z_rows)
        if fill is not None:
            from_y = after(from_y, *fill(own))
        return own + from_y.astype(f32) + from_z.astype(f32)

    def widened(weight, first, second):
        if group != 8:
            return lax.all_gather(
                weight, "fsdp", axis=1, tiled=True, axis_index_groups=strides
            )
        mine = after(own_part(weight, 4, 0, 1), first)
        theirs = swapped(mine, "fsdp", 4)
        theirs = shared(after(theirs, second))
        blocks = []
        for v in (0, 2, 1, 3):
            blocks += [own_part(weight, 4, v, 1), theirs[v]]
        return jnp.concatenate(blocks, axis=1)

    def replica_columns(pieces):
        size = pieces[0].shape[1]
        whole = jnp.zeros((pieces[0].shape[0], 4 * size), f32)
        for v, block in enumerate(pieces):
            start = (lax.axis_index("rep") ^ v) * size
            whole = lax.dynamic_update_slice_in_dim(whole, block.astype(f32), start, 1)
        return whole

    def send_terms(rows, units):
        return across(rows, units[:, units.shape[1] // 2 :]).astype(bf16)

    def keep_terms(rows, units, near):
        total = across(rows, units[:, : units.shape[1] // 2]) + near.astype(f32)
        half = total.shape[1] // 2
        return total[:, :half], total[:, half:].astype(bf16)

    def to_partner(kept, far):
        total = kept + far.astype(f32)
        half = total.shape[1] // 2
        return total[:, :half], total[:, half:].astype(bf16)

    def narrowed_whole(rows, units):
        total = lax.psum_scatter(
            across(rows, units).astype(bf16),
            "fsdp",
            scatter_dimension=1,
            tiled=True,
            axis_index_groups=strides,
        )
        return lax.psum(total, "rep").astype(f32)

    half = HEAD_DIM // 2
    frequency = rope_base ** (-(jnp.arange(half, dtype=f32) * (2.0 / HEAD_DIM)))
    angles = jnp.arange(SEQ, dtype=jnp.int32).astype(f32)[:, None] * frequency[None, :]
    cosine, sine = jnp.cos(angles), jnp.sin(angles)
    cosine = jnp.concatenate([cosine, cosine], axis=1)
    sine = jnp.concatenate([-sine, sine], axis=1)

    rows_weight = jnp.stack(
        [own_part(w, 4, 0, 0) for w in (query_weight, key_weight, value_weight)], axis=1
    )
    rows_weight = rows_weight.reshape(part, 3, chain, width).transpose(2, 0, 1, 3)
    rows_weight = rows_weight.reshape(chain, part, 3 * width)
    if group != chain:
        rows_weight = jnp.tile(rows_weight, (group // chain, 1, 1))
    columns_weight = lax.all_to_all(rows_weight, "fsdp", 0, 0)
    column_slots = shared(columns_weight)
    triple_weight = jnp.stack(in_order(column_slots), axis=1)
    triple_weight = triple_weight.reshape(model_width, 3 * width)
    all_tokens = of_sequence(tokens)

    own_gains = jnp.stack([query_norm, key_norm, mixer_norm, feeder_norm]).astype(f32)
    gains = lax.dynamic_update_slice_in_dim(
        jnp.zeros((4, model_width), f32), own_gains, me * shard, 1
    )
    gains = xor_sum(gains, "fsdp", group)
    if group == chain:
        pair_gains = own_gains[:2]
    else:
        pair_gains = lax.dynamic_slice_in_dim(gains[:2], spot * width, width, 1)
    mixer_gain = gains[2:3]
    feeder_gain = gains[3:4]

    pre = matmul(all_tokens, triple_weight)
    query_pre, key_pre = pre[:, :width], pre[:, width : 2 * width]
    squares = jnp.stack(
        [jnp.sum(query_pre * query_pre, axis=1), jnp.sum(key_pre * key_pre, axis=1)]
    )
    squares = xor_sum(squares, "fsdp", chain)
    query_low, key_low, value_low = prep(
        pre, squares, pair_gains.reshape(1, 2 * width), cosine, sine
    )
    mixed_low, mixed, log_total = attend(starts, query_low, key_low, value_low)
    output_piece = lax.all_gather(
        after(own_part(output_weight, 4, 0, 1), squares), "fsdp", axis=0, tiled=True
    )
    output_piece = after(output_piece, mixed_low)
    output_slots = shared(output_piece)
    whole_output = jnp.concatenate([output_slots[v] for v in (0, 2, 1, 3)], axis=1)

    mixed_rows = exchanged(mixed_low.reshape(chain, own_rows, width))
    mixed_rows = mixed_rows.transpose(1, 0, 2).reshape(own_rows, model_width)
    branch_near = matmul(mixed_rows, whole_output)
    quarter = model_width // 4
    branch_slots = [branch_near[:, i * quarter : (i + 1) * quarter] for i in (0, 2, 1, 3)]
    branch_pre = jnp.concatenate(in_order(branch_slots), axis=1)
    branch_factor = inverse_rms(branch_pre)
    hidden = tokens.astype(f32) + branch_pre * branch_factor * mixer_gain

    wide_gate = widened(gate_weight, squares, branch_near)
    wide_up = widened(up_weight, mixed_low, branch_near)
    all_hidden = of_quad(hidden.astype(bf16))
    gate = matmul(all_hidden, wide_gate).astype(bf16)
    wide_down = widened(down_weight, mixed_rows, gate)
    up = matmul(all_hidden, wide_up).astype(bf16)
    gate_wide, up_wide = gate.astype(f32), up.astype(f32)
    sigmoid = jax.nn.sigmoid(gate_wide)
    inner = (gate_wide * sigmoid * up_wide).astype(bf16)

    def down_terms(low, high, *deps):
        return against(after(inner[low:high], *deps), wide_down)

    down_pre = to_quad_rows(down_terms)
    down_factor = inverse_rms(down_pre)
    result = (hidden + down_pre * down_factor * feeder_gain).astype(bf16)

    tangent = cotangent.astype(f32)
    feeder_part = jnp.sum(tangent * down_pre * down_factor, axis=0)
    down_grad = norm_backward(down_pre, down_factor, feeder_gain, tangent).astype(bf16)
    all_down_grad = of_quad(down_grad)
    if group == 8:
        down_send = send_terms(all_down_grad, inner)
        down_near = swapped(down_send, "rep", 1)
        inner_grad = matmul(after(all_down_grad, down_send), wide_down)
    else:
        inner_grad = matmul(all_down_grad, wide_down)
    gate_grad = (
        inner_grad * up_wide * sigmoid * (1.0 + gate_wide * (1.0 - sigmoid))
    ).astype(bf16)
    up_grad = (inner_grad * gate_wide * sigmoid).astype(bf16)
    if group == 8:
        down_kept, down_pass = keep_terms(
            all_down_grad, after(inner, gate_grad, up_grad), down_near
        )
        down_far = swapped(down_pass, "rep", 2)
        back_gate, back_up = after(gate_grad, down_pass), after(up_grad, down_pass)
    else:
        back_gate, back_up = gate_grad, up_grad
    stage = {}

    def early_gradients(own):
        if group != 8:
            return ()
        late_gate = after(gate_grad, own)
        gate_send = send_terms(all_hidden, late_gate)
        gate_near = swapped(gate_send, "rep", 1)
        up_send = send_terms(all_hidden, after(up_grad, gate_send))
        stage["up_near"] = swapped(up_send, "rep", 1)
        gate_kept, gate_pass = keep_terms(
            all_hidden, after(gate_grad, up_send), gate_near
        )
        stage["gate"] = gate_kept, swapped(gate_pass, "rep", 2)
        return (gate_pass,)

    def back_terms(low, high, *deps):
        return against(after(back_gate[low:high], *deps), wide_gate) + against(
            after(back_up[low:high], *deps), wide_up
        )

    feed_back = to_quad_rows(back_terms, early_gradients)
    hidden_grad = tangent + feed_back
    mixer_part = jnp.sum(hidden_grad * branch_pre * branch_factor, axis=0)
    branch_grad = norm_backward(
        branch_pre, branch_factor, mixer_gain, hidden_grad
    ).astype(bf16)

    grad_near = jnp.concatenate(
        [own_part(branch_grad, 4, v, 1) for v in (0, 2, 1, 3)], axis=1
    )
    mixed_grad_rows = against(grad_near, whole_output).astype(bf16)
    mixed_grad_rows = mixed_grad_rows.reshape(own_rows, chain, width).transpose(1, 0, 2)
    mixed_grad = exchanged(mixed_grad_rows)
    mixed_grad = mixed_grad.reshape(chain * own_rows, width)
    output_half = model_width // 2
    late_rows = after(mixed_rows, mixed_grad_rows)
    output_send = across(late_rows, grad_near[:, output_half:]).astype(bf16)
    output_near = swapped(output_send, "rep", 1)
    late_rows = after(mixed_rows, output_send)
    if group == 8:
        late_up = after(up_grad, output_send)
        up_kept, up_pass = keep_terms(all_hidden, late_up, stage["up_near"])
        up_far = swapped(up_pass, "rep", 2)
        late_rows = after(mixed_rows, up_pass)
    output_kept = across(late_rows, grad_near[:, :output_half]) + output_near.astype(f32)
    output_pass = output_kept[:, quarter:].astype(bf16)
    output_kept = output_kept[:, :quarter]
    output_far = swapped(output_pass, "rep", 2)
    if group == 8:
        down_kept, down_pass = to_partner(down_kept, after(down_far, mixed_grad))
        down_theirs = swapped(down_pass, "fsdp", 4)
        mixed_grad = after(mixed_grad, output_pass)
    query_turn, key_turn, value_grad = attend_back(
        starts,
        query_low,
        mixed_grad,
        mixed,
        log_total,
        key_low,
        value_low,
        cosine,
        sine,
    )
    query_gain, key_gain = pair_gains[0:1], pair_gains[1:2]
    means = jnp.stack(
        [
            jnp.sum(query_gain * query_turn * query_pre, axis=1),
            jnp.sum(key_gain * key_turn * key_pre, axis=1),
        ]
    )
    factors = lax.rsqrt(squares * (1.0 / model_width) + norm_epsilon)

    def gain_part(turn, pre_part, at):
        own = jnp.sum(turn * pre_part * factors[at][:, None], axis=0)
        whole = jnp.zeros((model_width,), f32)
        return lax.dynamic_update_slice_in_dim(whole, own, spot * width, 0)

    gain_parts = jnp.stack(
        [
            gain_part(query_turn, query_pre, 0),
            gain_part(key_turn, key_pre, 1),
            mixer_part,
            feeder_part,
        ]
    )
    if group == chain and model_width == means.shape[1]:
        packed = xor_sum(jnp.concatenate([means, gain_parts]), "fsdp", group)
        means, gain_parts = packed[:2], packed[2:]
    else:
        means = xor_sum(means, "fsdp", chain)
        gain_parts = xor_sum(gain_parts, "fsdp", group)
    means = means * (1.0 / model_width)

    def pair_back(turn, pre_part, gain, at):
        factor = factors[at][:, None]
        grad = factor * gain * turn - pre_part * factor * factor * factor * means[at][:, None]
        return grad.astype(bf16)

    query_grad = pair_back(query_turn, query_pre, query_gain, 0)
    key_grad = pair_back(key_turn, key_pre, key_gain, 1)
    triple_grad = jnp.concatenate([query_grad, key_grad, value_grad], axis=1)
    if group == 8:
        down_total = (
            down_kept + after(down_theirs, triple_grad).astype(f32)
        ).astype(bf16)
        down_pieces = shared(down_total)
        gate_kept, gate_far = stage["gate"]
        gate_kept, gate_pass = to_partner(gate_kept, after(gate_far, triple_grad))
        gate_theirs = swapped(gate_pass, "fsdp", 4)
    token_terms = against(triple_grad, triple_weight).astype(bf16)
    token_rows = to_sequence_rows(token_terms)
    gradient_tokens = (hidden_grad + token_rows).astype(bf16)

    late_grad = after(triple_grad, token_terms)
    triple_part = across(all_tokens, late_grad)
    if group == chain:
        triple_part = triple_part.reshape(chain, 4, part, 3 * width)
        slots = [own_part(triple_part, 4, v, 1)[:, 0] for v in range(4)]
        sends = [slots[v].astype(bf16) for v in (3, 1)]
        near = [swapped(x, "rep", 1) for x in sends]
        passed = (slots[2] + near[0].astype(f32)).astype(bf16)
        kept = slots[0] + near[1].astype(f32)
        passed_far = swapped(passed, "rep", 2)
        if group == 8:
            up_kept, up_pass = to_partner(up_kept, after(up_far, passed))
            up_theirs = swapped(up_pass, "fsdp", 4)
            output_far = after(output_far, up_pass)
        output_terms = (output_kept + output_far.astype(f32)).astype(bf16)
        output_part = to_group_rows(output_terms).astype(bf16)
        passed_far = after(passed_far, output_terms)
        kept = (kept + passed_far.astype(f32)).astype(bf16)
        heads_rows = lax.all_to_all(kept, "fsdp", 0, 0)
        if group == 8:
            gate_theirs = after(gate_theirs, kept)
            gate_total = (gate_kept + gate_theirs.astype(f32)).astype(bf16)
            gate_pieces = shared(gate_total)
            heads_rows = after(heads_rows, gate_total)
        triple_pieces = shared(heads_rows)
        if group == 8:
            up_theirs = after(up_theirs, heads_rows)
            up_total = (up_kept + up_theirs.astype(f32)).astype(bf16)
            up_pieces = shared(up_total)
            output_part = after(output_part, up_total)
            gradient_down = replica_columns(down_pieces)
            gradient_gate = replica_columns(gate_pieces)
            gradient_up = replica_columns(up_pieces)
        output_pieces = shared(output_part)
        triple_rows = jnp.stack(in_order(triple_pieces))
        triple_rows = triple_rows.reshape(4, chain, part, 3, width)
        triple_rows = triple_rows.transpose(3, 0, 2, 1, 4).reshape(3, shard, model_width)
    else:
        output_terms = (output_kept + output_far.astype(f32)).astype(bf16)
        output_pieces = shared(to_group_rows(output_terms).astype(bf16))
        triple_rows = lax.dynamic_update_slice_in_dim(
            jnp.zeros((model_width, 3, chain, width), f32),
            triple_part.reshape(model_width, 3, 1, width),
            spot,
            2,
        )
        triple_rows = to_group_rows(triple_rows.reshape(model_width, 3 * model_width))
        triple_rows = lax.psum(triple_rows.astype(bf16), "rep")
        triple_rows = triple_rows.reshape(shard, 3, model_width).transpose(1, 0, 2)
    gradient_output = replica_columns(output_pieces)
    if group != 8:
        gradient_down = narrowed_whole(all_down_grad, inner)
        gradient_gate = narrowed_whole(all_hidden, gate_grad)
        gradient_up = narrowed_whole(all_hidden, up_grad)
    triple_rows = triple_rows.astype(f32)

    gain_parts = xor_sum(gain_parts, "rep", 4)
    gain_own = lax.dynamic_slice_in_dim(gain_parts, me * shard, shard, 1)
    return (
        result,
        gradient_tokens,
        triple_rows[0],
        triple_rows[1],
        triple_rows[2],
        gain_own[0],
        gain_own[1],
        gradient_output,
        gain_own[2],
        gradient_gate,
        gradient_up,
        gradient_down,
        gain_own[3],
    )


def solution(mesh):
    rows, ends = P(("rep", "fsdp"), None), P(None, "fsdp")
    tops, line = P("fsdp", None), P("fsdp")
    return jax.shard_map(
        body,
        mesh=mesh,
        in_specs=(
            rows, tops, tops, tops, line, line, tops, line, ends, ends, ends, line, P(), rows,
        ),
        out_specs=(
            rows, rows, tops, tops, tops, line, line, tops, line, ends, ends, ends, line,
        ),
        check_vma=False,
    )
```

```python
import jax
import jax.numpy as jnp
from jax import lax
from jax.experimental import pallas as pl
from jax.experimental.pallas import tpu as pltpu
from jax.sharding import PartitionSpec as P

HEADS = 16
HEAD_DIM = 128
SEQ = 2048
PIECE = 256
BLOCK = 512

norm_epsilon = 1e-06
rope_base = 500000.0
masked_score = -1e30
score_factor = HEAD_DIM ** (-0.5)
f32 = jnp.float32
bf16 = jnp.bfloat16


def matmul(a, b):
    return jnp.dot(a, b, preferred_element_type=f32)


def against(a, b):
    return lax.dot_general(a, b, (((1,), (1,)), ((), ())), preferred_element_type=f32)


def across(a, b):
    return lax.dot_general(a, b, (((0,), (0,)), ((), ())), preferred_element_type=f32)


def inverse_rms(values):
    return lax.rsqrt(jnp.mean(values * values, axis=-1, keepdims=True) + norm_epsilon)


def norm_backward(values, factor, gain_row, upstream):
    weighted = upstream * gain_row
    inner_mean = jnp.mean(weighted * values, axis=-1, keepdims=True)
    return factor * weighted - values * (factor * factor * factor) * inner_mean


def swapped(block, axis, bit):
    size = lax.axis_size(axis)
    return lax.ppermute(block, axis, [(i, i ^ bit) for i in range(size)])


def after(block, *others):
    return lax.optimization_barrier((block,) + others)[0]


def xor_sum(block, axis, size):
    bit = 1
    while bit < size:
        block = block + swapped(block, axis, bit)
        bit *= 2
    return block


def replica_bits():
    me = lax.axis_index("rep")
    return (me & 1) == 1, (me & 2) == 2


def shared(piece):
    far = swapped(piece, "rep", 2)
    near = swapped(piece, "rep", 1)
    return [piece, near, far, swapped(far, "rep", 1)]


def in_order(slots):
    odd, high = replica_bits()
    paired = [jnp.where(odd, slots[v ^ 1], slots[v]) for v in range(4)]
    return [jnp.where(high, paired[q ^ 2], paired[q]) for q in range(4)]


def own_part(block, count, which, axis):
    size = block.shape[axis] // count
    start = (lax.axis_index("rep") ^ which) * size
    return lax.dynamic_slice_in_dim(block, start, size, axis)


def piece_label(places, starts_ref):
    label = jnp.where((places >= starts_ref[0]) & (places < starts_ref[0] + PIECE), 1, 0)
    for j in range(1, starts_ref.shape[0]):
        inside = (places >= starts_ref[j]) & (places < starts_ref[j] + PIECE)
        label = jnp.where(inside, j + 1, label)
    return label


def allowed_block(starts_ref, query_start, query_count, key_start, key_count):
    query_places = query_start + lax.broadcasted_iota(jnp.int32, (query_count, 1), 0)
    key_places = key_start + lax.broadcasted_iota(jnp.int32, (1, key_count), 1)
    query_labels = piece_label(query_places, starts_ref)
    key_labels = piece_label(key_places, starts_ref)
    return (key_places <= query_places) | (
        (query_labels == key_labels) & (query_labels > 0)
    )


def straddles(starts_ref, edge):
    hit = jnp.int32(0)
    for j in range(starts_ref.shape[0]):
        begin = starts_ref[j]
        hit = jnp.where((begin < edge) & (begin + PIECE > edge), 1, hit)
    return hit


def prep_kernel(pre_ref, square_ref, gain_ref, cos_ref, sin_ref, q_ref, k_ref, v_ref):
    rows = pre_ref.shape[0]
    width = q_ref.shape[1]
    cosine, sine = cos_ref[...], sin_ref[...]
    for which, out_ref in ((0, q_ref), (1, k_ref)):
        square = jnp.broadcast_to(square_ref[which : which + 1, :], (HEAD_DIM, rows)).T
        factor = lax.rsqrt(square * (1.0 / (HEADS * HEAD_DIM)) + norm_epsilon)
        for at in range(0, width, HEAD_DIM):
            low, high = which * width + at, which * width + at + HEAD_DIM
            x = pre_ref[:, low:high] * factor * gain_ref[:, low:high]
            x = x * cosine + pltpu.roll(x, HEAD_DIM // 2, 1) * sine
            out_ref[:, at : at + HEAD_DIM] = x.astype(bf16)
    v_ref[...] = pre_ref[:, 2 * width :].astype(bf16)


def prep(pre, square, gains, cosine, sine):
    rows, triple = pre.shape
    width = triple // 3
    step = 512
    return pl.pallas_call(
        prep_kernel,
        grid=(rows // step,),
        in_specs=[
            pl.BlockSpec((step, triple), lambda i: (i, 0)),
            pl.BlockSpec((2, step), lambda i: (0, i)),
            pl.BlockSpec((1, 2 * width), lambda i: (0, 0)),
            pl.BlockSpec((step, HEAD_DIM), lambda i: (i, 0)),
            pl.BlockSpec((step, HEAD_DIM), lambda i: (i, 0)),
        ],
        out_specs=[pl.BlockSpec((step, width), lambda i: (i, 0))] * 3,
        out_shape=[jax.ShapeDtypeStruct((rows, width), bf16)] * 3,
        cost_estimate=pl.CostEstimate(
            flops=rows * triple * 8, bytes_accessed=rows * triple * 6, transcendentals=0
        ),
        name="prep",
    )(pre, square, gains, cosine, sine)


def attend_kernel(starts_ref, q_ref, k_ref, v_ref, low_ref, mixed_ref, total_ref):
    at = pl.program_id(1)
    query = q_ref[...]
    rows = query.shape[0]

    def step(carry, key_start, key_count, masked):
        row_max, row_sum, mixed = carry
        key = k_ref[pl.ds(key_start, key_count), :]
        value = v_ref[pl.ds(key_start, key_count), :]
        scores = against(query, key) * score_factor
        if masked:
            allowed = allowed_block(starts_ref, at * rows, rows, key_start, key_count)
            scores = jnp.where(allowed, scores, masked_score)
        new_max = jnp.maximum(row_max, jnp.max(scores, axis=1, keepdims=True))
        fade = jnp.exp(row_max - new_max)
        exponent = jnp.exp(scores - new_max)
        row_sum = row_sum * fade + jnp.sum(exponent, axis=1, keepdims=True)
        mixed = mixed * fade + matmul(exponent.astype(bf16), value)
        return new_max, row_sum, mixed

    carry = (
        jnp.full((rows, 1), masked_score, f32),
        jnp.zeros((rows, 1), f32),
        jnp.zeros((rows, HEAD_DIM), f32),
    )
    carry = step(carry, pl.multiple_of(at * rows, rows), rows, True)
    carry = lax.fori_loop(
        0,
        at,
        lambda j, c: step(c, pl.multiple_of(j * rows, rows), rows, False),
        carry,
    )
    edge = (at + 1) * rows
    carry = lax.fori_loop(
        0,
        straddles(starts_ref, edge),
        lambda j, c: step(c, pl.multiple_of(edge, rows), PIECE, True),
        carry,
    )
    row_max, row_sum, mixed = carry
    mixed = mixed / row_sum
    low_ref[...] = mixed.astype(bf16)
    mixed_ref[...] = mixed
    total_ref[...] = jnp.broadcast_to(row_max + jnp.log(row_sum), (rows, HEAD_DIM))


def attend(starts, query, key, value):
    rows, width = query.shape
    heads = width // HEAD_DIM
    block = pl.BlockSpec((BLOCK, HEAD_DIM), lambda h, i, s: (i, h))
    column = pl.BlockSpec((rows, HEAD_DIM), lambda h, i, s: (0, h))
    return pl.pallas_call(
        attend_kernel,
        grid_spec=pltpu.PrefetchScalarGridSpec(
            num_scalar_prefetch=1,
            grid=(heads, rows // BLOCK),
            in_specs=[block, column, column],
            out_specs=[block, block, block],
        ),
        out_shape=[
            jax.ShapeDtypeStruct((rows, width), bf16),
            jax.ShapeDtypeStruct((rows, width), f32),
            jax.ShapeDtypeStruct((rows, width), f32),
        ],
        cost_estimate=pl.CostEstimate(
            flops=heads * rows * rows * HEAD_DIM * 2,
            bytes_accessed=rows * width * 16,
            transcendentals=heads * rows * rows // 2,
        ),
        name="attend",
    )(starts, query, key, value)


def attend_back_kernel(
    starts_ref,
    q_ref,
    grad_ref,
    mixed_ref,
    total_ref,
    k_ref,
    v_ref,
    cos_ref,
    sin_ref,
    dq_ref,
    dk_ref,
    dv_ref,
    dv_total,
):
    at = pl.program_id(1)
    query = q_ref[...]
    grad = grad_ref[...]
    rows = query.shape[0]
    total = total_ref[:, 0:1]
    inner = jnp.sum(grad.astype(f32) * mixed_ref[...], axis=1, keepdims=True)

    @pl.when(at == 0)
    def _():
        dk_ref[...] = jnp.zeros_like(dk_ref)
        dv_total[...] = jnp.zeros_like(dv_total)

    def step(dq, key_start, key_count, masked):
        here = pl.ds(key_start, key_count)
        key = k_ref[here, :]
        value = v_ref[here, :]
        scores = against(query, key) * score_factor
        if masked:
            allowed = allowed_block(starts_ref, at * rows, rows, key_start, key_count)
            scores = jnp.where(allowed, scores, masked_score)
        shares = jnp.exp(scores - total)
        share_grad = against(grad, value)
        score_grad = (shares * (share_grad - inner)).astype(bf16)
        dk_ref[here, :] += across(score_grad, query)
        dv_total[here, :] += across(shares.astype(bf16), grad)
        return dq + matmul(score_grad, key)

    dq = jnp.zeros((rows, HEAD_DIM), f32)
    dq = step(dq, pl.multiple_of(at * rows, rows), rows, True)
    dq = lax.fori_loop(
        0, at, lambda j, c: step(c, pl.multiple_of(j * rows, rows), rows, False), dq
    )
    edge = (at + 1) * rows
    dq = lax.fori_loop(
        0,
        straddles(starts_ref, edge),
        lambda j, c: step(c, pl.multiple_of(edge, rows), PIECE, True),
        dq,
    )

    def unrotated(x, cosine, sine):
        x = x * score_factor
        return x * cosine - pltpu.roll(x, HEAD_DIM // 2, 1) * sine

    mine = pl.ds(pl.multiple_of(at * rows, rows), rows)
    dq_ref[...] = unrotated(dq, cos_ref[mine, :], sin_ref[mine, :])

    @pl.when(at == pl.num_programs(1) - 1)
    def _():
        dk_ref[...] = unrotated(dk_ref[...], cos_ref[...], sin_ref[...])
        dv_ref[...] = dv_total[...].astype(bf16)


def attend_back(starts, query, grad, mixed, total, key, value, cosine, sine):
    rows, width = query.shape
    heads = width // HEAD_DIM
    block = pl.BlockSpec((BLOCK, HEAD_DIM), lambda h, i, s: (i, h))
    column = pl.BlockSpec((rows, HEAD_DIM), lambda h, i, s: (0, h))
    table = pl.BlockSpec((rows, HEAD_DIM), lambda h, i, s: (0, 0))
    return pl.pallas_call(
        attend_back_kernel,
        grid_spec=pltpu.PrefetchScalarGridSpec(
            num_scalar_prefetch=1,
            grid=(heads, rows // BLOCK),
            in_specs=[block, block, block, block, column, column, table, table],
            out_specs=[block, column, column],
            scratch_shapes=[pltpu.VMEM((rows, HEAD_DIM), f32)],
        ),
        out_shape=[
            jax.ShapeDtypeStruct((rows, width), f32),
            jax.ShapeDtypeStruct((rows, width), f32),
            jax.ShapeDtypeStruct((rows, width), bf16),
        ],
        cost_estimate=pl.CostEstimate(
            flops=heads * rows * rows * HEAD_DIM * 5,
            bytes_accessed=rows * width * 28,
            transcendentals=heads * rows * rows // 2,
        ),
        name="attend_back",
    )(starts, query, grad, mixed, total, key, value, cosine, sine)


def body(
    tokens,
    query_weight,
    key_weight,
    value_weight,
    query_norm,
    key_norm,
    output_weight,
    mixer_norm,
    gate_weight,
    up_weight,
    down_weight,
    feeder_norm,
    piece_starts,
    cotangent,
):
    own_rows, model_width = tokens.shape
    group = lax.axis_size("fsdp")
    assert lax.axis_size("rep") == 4 and group % 4 == 0
    me = lax.axis_index("fsdp")
    chain = SEQ // own_rows
    spot = me % chain
    width = model_width // chain
    shard = model_width // group
    part = shard // 4
    sequence = ((lax.axis_index("rep") * group + me) * own_rows) // SEQ
    starts = lax.dynamic_index_in_dim(piece_starts, sequence, 0, keepdims=False)
    teams = None
    if group != chain:
        teams = [[b * chain + i for i in range(chain)] for b in range(group // chain)]
    strides = [[r + 4 * m for m in range(group // 4)] for r in range(4)]

    def of_sequence(block):
        return lax.all_gather(block, "fsdp", axis=0, tiled=True, axis_index_groups=teams)

    def to_sequence_rows(block):
        return lax.psum_scatter(
            block.astype(bf16),
            "fsdp",
            scatter_dimension=0,
            tiled=True,
            axis_index_groups=teams,
        ).astype(f32)

    def to_group_rows(block):
        return lax.psum_scatter(
            block.astype(bf16), "fsdp", scatter_dimension=0, tiled=True
        ).astype(f32)

    def exchanged(block):
        return lax.all_to_all(block, "fsdp", 0, 0, axis_index_groups=teams)

    def of_quad(block):
        half = block.shape[0] // 2
        along_y = swapped(block, "fsdp", 1)
        along_z = swapped(block, "fsdp", 2)
        top = swapped(along_y[:half], "fsdp", 2)
        bottom = swapped(along_z[half:], "fsdp", 1)
        return jnp.concatenate([block, along_y, along_z, top, bottom])

    def to_quad_rows(terms, fill=None):
        half = own_rows // 2
        across_rows = terms(3 * own_rows, 4 * own_rows).astype(bf16)
        top = swapped(across_rows[:half], "fsdp", 2)
        bottom = swapped(across_rows[half:], "fsdp", 1)
        middle = terms(own_rows, 3 * own_rows)
        y_rows = jnp.concatenate(
            [middle[:half] + top.astype(f32), middle[half:own_rows]]
        ).astype(bf16)
        z_rows = jnp.concatenate(
            [
                middle[own_rows : own_rows + half],
                middle[own_rows + half :] + bottom.astype(f32),
            ]
        ).astype(bf16)
        from_y = swapped(y_rows, "fsdp", 1)
        from_z = swapped(z_rows, "fsdp", 2)
        own = terms(0, own_rows, y_rows, z_rows)
        if fill is not None:
            from_y = after(from_y, *fill(own))
        return own + from_y.astype(f32) + from_z.astype(f32)

    def widened(weight, first, second):
        if group != 8:
            return lax.all_gather(
                weight, "fsdp", axis=1, tiled=True, axis_index_groups=strides
            )
        mine = after(own_part(weight, 4, 0, 1), first)
        theirs = swapped(mine, "fsdp", 4)
        theirs = shared(after(theirs, second))
        blocks = []
        for v in (0, 2, 1, 3):
            blocks += [own_part(weight, 4, v, 1), theirs[v]]
        return jnp.concatenate(blocks, axis=1)

    def replica_columns(pieces):
        size = pieces[0].shape[1]
        whole = jnp.zeros((pieces[0].shape[0], 4 * size), f32)
        for v, block in enumerate(pieces):
            start = (lax.axis_index("rep") ^ v) * size
            whole = lax.dynamic_update_slice_in_dim(whole, block.astype(f32), start, 1)
        return whole

    def send_terms(rows, units):
        return across(rows, units[:, units.shape[1] // 2 :]).astype(bf16)

    def keep_terms(rows, units, near):
        total = across(rows, units[:, : units.shape[1] // 2]) + near.astype(f32)
        half = total.shape[1] // 2
        return total[:, :half], total[:, half:].astype(bf16)

    def to_partner(kept, far):
        total = kept + far.astype(f32)
        half = total.shape[1] // 2
        return total[:, :half], total[:, half:].astype(bf16)

    def narrowed_whole(rows, units):
        total = lax.psum_scatter(
            across(rows, units).astype(bf16),
            "fsdp",
            scatter_dimension=1,
            tiled=True,
            axis_index_groups=strides,
        )
        return lax.psum(total, "rep").astype(f32)

    half = HEAD_DIM // 2
    frequency = rope_base ** (-(jnp.arange(half, dtype=f32) * (2.0 / HEAD_DIM)))
    angles = jnp.arange(SEQ, dtype=jnp.int32).astype(f32)[:, None] * frequency[None, :]
    cosine, sine = jnp.cos(angles), jnp.sin(angles)
    cosine = jnp.concatenate([cosine, cosine], axis=1)
    sine = jnp.concatenate([-sine, sine], axis=1)

    rows_weight = jnp.stack(
        [own_part(w, 4, 0, 0) for w in (query_weight, key_weight, value_weight)], axis=1
    )
    rows_weight = rows_weight.reshape(part, 3, chain, width).transpose(2, 0, 1, 3)
    rows_weight = rows_weight.reshape(chain, part, 3 * width)
    if group != chain:
        rows_weight = jnp.tile(rows_weight, (group // chain, 1, 1))
    columns_weight = lax.all_to_all(rows_weight, "fsdp", 0, 0)
    column_slots = shared(columns_weight)
    triple_weight = jnp.stack(in_order(column_slots), axis=1)
    triple_weight = triple_weight.reshape(model_width, 3 * width)
    all_tokens = of_sequence(tokens)

    own_gains = jnp.stack([query_norm, key_norm, mixer_norm, feeder_norm]).astype(f32)
    gains = lax.dynamic_update_slice_in_dim(
        jnp.zeros((4, model_width), f32), own_gains, me * shard, 1
    )
    gains = xor_sum(gains, "fsdp", group)
    if group == chain:
        pair_gains = own_gains[:2]
    else:
        pair_gains = lax.dynamic_slice_in_dim(gains[:2], spot * width, width, 1)
    mixer_gain = gains[2:3]
    feeder_gain = gains[3:4]

    pre = matmul(all_tokens, triple_weight)
    query_pre, key_pre = pre[:, :width], pre[:, width : 2 * width]
    squares = jnp.stack(
        [jnp.sum(query_pre * query_pre, axis=1), jnp.sum(key_pre * key_pre, axis=1)]
    )
    squares = xor_sum(squares, "fsdp", chain)
    query_low, key_low, value_low = prep(
        pre, squares, pair_gains.reshape(1, 2 * width), cosine, sine
    )
    mixed_low, mixed, log_total = attend(starts, query_low, key_low, value_low)
    output_piece = lax.all_gather(
        after(own_part(output_weight, 4, 0, 1), squares), "fsdp", axis=0, tiled=True
    )
    output_piece = after(output_piece, mixed_low)
    output_slots = shared(output_piece)
    whole_output = jnp.concatenate([output_slots[v] for v in (0, 2, 1, 3)], axis=1)

    mixed_rows = exchanged(mixed_low.reshape(chain, own_rows, width))
    mixed_rows = mixed_rows.transpose(1, 0, 2).reshape(own_rows, model_width)
    branch_near = matmul(mixed_rows, whole_output)
    quarter = model_width // 4
    branch_slots = [branch_near[:, i * quarter : (i + 1) * quarter] for i in (0, 2, 1, 3)]
    branch_pre = jnp.concatenate(in_order(branch_slots), axis=1)
    branch_factor = inverse_rms(branch_pre)
    hidden = tokens.astype(f32) + branch_pre * branch_factor * mixer_gain

    wide_gate = widened(gate_weight, mixed_low, branch_near)
    wide_up = widened(up_weight, mixed_rows, branch_near)
    all_hidden = of_quad(hidden.astype(bf16))
    gate = matmul(all_hidden, wide_gate).astype(bf16)
    wide_down = widened(down_weight, mixed_rows, gate)
    up = matmul(all_hidden, wide_up).astype(bf16)
    gate_wide, up_wide = gate.astype(f32), up.astype(f32)
    sigmoid = jax.nn.sigmoid(gate_wide)
    inner = (gate_wide * sigmoid * up_wide).astype(bf16)

    def down_terms(low, high, *deps):
        return against(after(inner[low:high], *deps), wide_down)

    down_pre = to_quad_rows(down_terms)
    down_factor = inverse_rms(down_pre)
    result = (hidden + down_pre * down_factor * feeder_gain).astype(bf16)

    tangent = cotangent.astype(f32)
    feeder_part = jnp.sum(tangent * down_pre * down_factor, axis=0)
    down_grad = norm_backward(down_pre, down_factor, feeder_gain, tangent).astype(bf16)
    all_down_grad = of_quad(down_grad)
    if group == 8:
        down_send = send_terms(all_down_grad, inner)
        down_near = swapped(down_send, "rep", 1)
        inner_grad = matmul(after(all_down_grad, down_send), wide_down)
    else:
        inner_grad = matmul(all_down_grad, wide_down)
    gate_grad = (
        inner_grad * up_wide * sigmoid * (1.0 + gate_wide * (1.0 - sigmoid))
    ).astype(bf16)
    up_grad = (inner_grad * gate_wide * sigmoid).astype(bf16)
    if group == 8:
        down_kept, down_pass = keep_terms(
            all_down_grad, after(inner, gate_grad, up_grad), down_near
        )
        down_far = swapped(down_pass, "rep", 2)
        back_gate, back_up = after(gate_grad, down_pass), after(up_grad, down_pass)
    else:
        back_gate, back_up = gate_grad, up_grad
    stage = {}

    def early_gradients(own):
        if group != 8:
            return ()
        late_gate = after(gate_grad, own)
        gate_send = send_terms(all_hidden, late_gate)
        gate_near = swapped(gate_send, "rep", 1)
        up_send = send_terms(all_hidden, after(up_grad, gate_send))
        stage["up_near"] = swapped(up_send, "rep", 1)
        gate_kept, gate_pass = keep_terms(
            all_hidden, after(gate_grad, up_send), gate_near
        )
        stage["gate"] = gate_kept, swapped(gate_pass, "rep", 2)
        return (gate_pass,)

    def back_terms(low, high, *deps):
        return against(after(back_gate[low:high], *deps), wide_gate) + against(
            after(back_up[low:high], *deps), wide_up
        )

    feed_back = to_quad_rows(back_terms, early_gradients)
    hidden_grad = tangent + feed_back
    mixer_part = jnp.sum(hidden_grad * branch_pre * branch_factor, axis=0)
    branch_grad = norm_backward(
        branch_pre, branch_factor, mixer_gain, hidden_grad
    ).astype(bf16)

    grad_near = jnp.concatenate(
        [own_part(branch_grad, 4, v, 1) for v in (0, 2, 1, 3)], axis=1
    )
    mixed_grad_rows = against(grad_near, whole_output).astype(bf16)
    mixed_grad_rows = mixed_grad_rows.reshape(own_rows, chain, width).transpose(1, 0, 2)
    mixed_grad = exchanged(mixed_grad_rows)
    mixed_grad = mixed_grad.reshape(chain * own_rows, width)
    output_half = model_width // 2
    late_rows = after(mixed_rows, mixed_grad_rows)
    output_send = across(late_rows, grad_near[:, output_half:]).astype(bf16)
    output_near = swapped(output_send, "rep", 1)
    late_rows = after(mixed_rows, output_send)
    if group == 8:
        late_up = after(up_grad, output_send)
        up_kept, up_pass = keep_terms(all_hidden, late_up, stage["up_near"])
        up_far = swapped(up_pass, "rep", 2)
        late_rows = after(mixed_rows, up_pass)
    output_kept = across(late_rows, grad_near[:, :output_half]) + output_near.astype(f32)
    output_pass = output_kept[:, quarter:].astype(bf16)
    output_kept = output_kept[:, :quarter]
    output_far = swapped(output_pass, "rep", 2)
    if group == 8:
        down_kept, down_pass = to_partner(down_kept, after(down_far, mixed_grad))
        down_theirs = swapped(down_pass, "fsdp", 4)
        mixed_grad = after(mixed_grad, output_pass)
    query_turn, key_turn, value_grad = attend_back(
        starts,
        query_low,
        mixed_grad,
        mixed,
        log_total,
        key_low,
        value_low,
        cosine,
        sine,
    )
    query_gain, key_gain = pair_gains[0:1], pair_gains[1:2]
    means = jnp.stack(
        [
            jnp.sum(query_gain * query_turn * query_pre, axis=1),
            jnp.sum(key_gain * key_turn * key_pre, axis=1),
        ]
    )
    factors = lax.rsqrt(squares * (1.0 / model_width) + norm_epsilon)

    def gain_part(turn, pre_part, at):
        own = jnp.sum(turn * pre_part * factors[at][:, None], axis=0)
        whole = jnp.zeros((model_width,), f32)
        return lax.dynamic_update_slice_in_dim(whole, own, spot * width, 0)

    gain_parts = jnp.stack(
        [
            gain_part(query_turn, query_pre, 0),
            gain_part(key_turn, key_pre, 1),
            mixer_part,
            feeder_part,
        ]
    )
    if group == chain and model_width == means.shape[1]:
        packed = xor_sum(jnp.concatenate([means, gain_parts]), "fsdp", group)
        means, gain_parts = packed[:2], packed[2:]
    else:
        means = xor_sum(means, "fsdp", chain)
        gain_parts = xor_sum(gain_parts, "fsdp", group)
    means = means * (1.0 / model_width)

    def pair_back(turn, pre_part, gain, at):
        factor = factors[at][:, None]
        grad = factor * gain * turn - pre_part * factor * factor * factor * means[at][:, None]
        return grad.astype(bf16)

    query_grad = pair_back(query_turn, query_pre, query_gain, 0)
    key_grad = pair_back(key_turn, key_pre, key_gain, 1)
    triple_grad = jnp.concatenate([query_grad, key_grad, value_grad], axis=1)
    if group == 8:
        down_total = (
            down_kept + after(down_theirs, triple_grad).astype(f32)
        ).astype(bf16)
        down_pieces = shared(down_total)
        gate_kept, gate_far = stage["gate"]
        gate_kept, gate_pass = to_partner(gate_kept, after(gate_far, triple_grad))
        gate_theirs = swapped(gate_pass, "fsdp", 4)
    token_terms = against(triple_grad, triple_weight).astype(bf16)
    token_rows = to_sequence_rows(token_terms)
    gradient_tokens = (hidden_grad + token_rows).astype(bf16)

    late_grad = after(triple_grad, token_terms)
    triple_part = across(all_tokens, late_grad)
    if group == chain:
        triple_part = triple_part.reshape(chain, 4, part, 3 * width)
        slots = [own_part(triple_part, 4, v, 1)[:, 0] for v in range(4)]
        sends = [slots[v].astype(bf16) for v in (3, 1)]
        near = [swapped(x, "rep", 1) for x in sends]
        passed = (slots[2] + near[0].astype(f32)).astype(bf16)
        kept = slots[0] + near[1].astype(f32)
        passed_far = swapped(passed, "rep", 2)
        if group == 8:
            up_kept, up_pass = to_partner(up_kept, after(up_far, passed))
            up_theirs = swapped(up_pass, "fsdp", 4)
            output_far = after(output_far, up_pass)
        output_terms = (output_kept + output_far.astype(f32)).astype(bf16)
        output_part = lax.all_to_all(
            output_terms.reshape(group, shard, quarter), "fsdp", 0, 0
        )
        output_part = jnp.sum(output_part.astype(f32), axis=0).astype(bf16)
        passed_far = after(passed_far, output_terms)
        kept = (kept + passed_far.astype(f32)).astype(bf16)
        heads_rows = lax.all_to_all(kept, "fsdp", 0, 0)
        if group == 8:
            gate_theirs = after(gate_theirs, kept)
            gate_total = (gate_kept + gate_theirs.astype(f32)).astype(bf16)
            gate_pieces = shared(gate_total)
            heads_rows = after(heads_rows, gate_total)
        triple_pieces = shared(heads_rows)
        if group == 8:
            up_theirs = after(up_theirs, heads_rows)
            up_total = (up_kept + up_theirs.astype(f32)).astype(bf16)
            up_pieces = shared(up_total)
            output_part = after(output_part, up_total)
            gradient_down = replica_columns(down_pieces)
            gradient_gate = replica_columns(gate_pieces)
            gradient_up = replica_columns(up_pieces)
        output_pieces = shared(output_part)
        triple_rows = jnp.stack(in_order(triple_pieces))
        triple_rows = triple_rows.reshape(4, chain, part, 3, width)
        triple_rows = triple_rows.transpose(3, 0, 2, 1, 4).reshape(3, shard, model_width)
    else:
        output_terms = (output_kept + output_far.astype(f32)).astype(bf16)
        output_pieces = shared(to_group_rows(output_terms).astype(bf16))
        triple_rows = lax.dynamic_update_slice_in_dim(
            jnp.zeros((model_width, 3, chain, width), f32),
            triple_part.reshape(model_width, 3, 1, width),
            spot,
            2,
        )
        triple_rows = to_group_rows(triple_rows.reshape(model_width, 3 * model_width))
        triple_rows = lax.psum(triple_rows.astype(bf16), "rep")
        triple_rows = triple_rows.reshape(shard, 3, model_width).transpose(1, 0, 2)
    gradient_output = replica_columns(output_pieces)
    if group != 8:
        gradient_down = narrowed_whole(all_down_grad, inner)
        gradient_gate = narrowed_whole(all_hidden, gate_grad)
        gradient_up = narrowed_whole(all_hidden, up_grad)
    triple_rows = triple_rows.astype(f32)

    gain_parts = xor_sum(gain_parts, "rep", 4)
    gain_own = lax.dynamic_slice_in_dim(gain_parts, me * shard, shard, 1)
    return (
        result,
        gradient_tokens,
        triple_rows[0],
        triple_rows[1],
        triple_rows[2],
        gain_own[0],
        gain_own[1],
        gradient_output,
        gain_own[2],
        gradient_gate,
        gradient_up,
        gradient_down,
        gain_own[3],
    )


def solution(mesh):
    rows, ends = P(("rep", "fsdp"), None), P(None, "fsdp")
    tops, line = P("fsdp", None), P("fsdp")
    return jax.shard_map(
        body,
        mesh=mesh,
        in_specs=(
            rows, tops, tops, tops, line, line, tops, line, ends, ends, ends, line, P(), rows,
        ),
        out_specs=(
            rows, rows, tops, tops, tops, line, line, tops, line, ends, ends, ends, line,
        ),
        check_vma=False,
    )
```

```python
import jax
import jax.numpy as jnp
from jax import lax
from jax.experimental import pallas as pl
from jax.experimental.pallas import tpu as pltpu
from jax.sharding import PartitionSpec as P

HEADS = 16
HEAD_DIM = 128
SEQ = 2048
PIECE = 256
BLOCK = 512

norm_epsilon = 1e-06
rope_base = 500000.0
masked_score = -1e30
score_factor = HEAD_DIM ** (-0.5)
f32 = jnp.float32
bf16 = jnp.bfloat16


def matmul(a, b):
    return jnp.dot(a, b, preferred_element_type=f32)


def against(a, b):
    return lax.dot_general(a, b, (((1,), (1,)), ((), ())), preferred_element_type=f32)


def across(a, b):
    return lax.dot_general(a, b, (((0,), (0,)), ((), ())), preferred_element_type=f32)


def inverse_rms(values):
    return lax.rsqrt(jnp.mean(values * values, axis=-1, keepdims=True) + norm_epsilon)


def norm_backward(values, factor, gain_row, upstream):
    weighted = upstream * gain_row
    inner_mean = jnp.mean(weighted * values, axis=-1, keepdims=True)
    return factor * weighted - values * (factor * factor * factor) * inner_mean


def swapped(block, axis, bit):
    size = lax.axis_size(axis)
    return lax.ppermute(block, axis, [(i, i ^ bit) for i in range(size)])


def after(block, *others):
    return lax.optimization_barrier((block,) + others)[0]


def xor_sum(block, axis, size):
    bit = 1
    while bit < size:
        block = block + swapped(block, axis, bit)
        bit *= 2
    return block


def replica_bits():
    me = lax.axis_index("rep")
    return (me & 1) == 1, (me & 2) == 2


def shared(piece):
    far = swapped(piece, "rep", 2)
    near = swapped(piece, "rep", 1)
    return [piece, near, far, swapped(far, "rep", 1)]


def in_order(slots):
    odd, high = replica_bits()
    paired = [jnp.where(odd, slots[v ^ 1], slots[v]) for v in range(4)]
    return [jnp.where(high, paired[q ^ 2], paired[q]) for q in range(4)]


def own_part(block, count, which, axis):
    size = block.shape[axis] // count
    start = (lax.axis_index("rep") ^ which) * size
    return lax.dynamic_slice_in_dim(block, start, size, axis)


def piece_label(places, starts_ref):
    label = jnp.where((places >= starts_ref[0]) & (places < starts_ref[0] + PIECE), 1, 0)
    for j in range(1, starts_ref.shape[0]):
        inside = (places >= starts_ref[j]) & (places < starts_ref[j] + PIECE)
        label = jnp.where(inside, j + 1, label)
    return label


def allowed_block(starts_ref, query_start, query_count, key_start, key_count):
    query_places = query_start + lax.broadcasted_iota(jnp.int32, (query_count, 1), 0)
    key_places = key_start + lax.broadcasted_iota(jnp.int32, (1, key_count), 1)
    query_labels = piece_label(query_places, starts_ref)
    key_labels = piece_label(key_places, starts_ref)
    return (key_places <= query_places) | (
        (query_labels == key_labels) & (query_labels > 0)
    )


def straddles(starts_ref, edge):
    hit = jnp.int32(0)
    for j in range(starts_ref.shape[0]):
        begin = starts_ref[j]
        hit = jnp.where((begin < edge) & (begin + PIECE > edge), 1, hit)
    return hit


def prep_kernel(pre_ref, square_ref, gain_ref, cos_ref, sin_ref, q_ref, k_ref, v_ref):
    rows = pre_ref.shape[0]
    width = q_ref.shape[1]
    cosine, sine = cos_ref[...], sin_ref[...]
    for which, out_ref in ((0, q_ref), (1, k_ref)):
        square = jnp.broadcast_to(square_ref[which : which + 1, :], (HEAD_DIM, rows)).T
        factor = lax.rsqrt(square * (1.0 / (HEADS * HEAD_DIM)) + norm_epsilon)
        for at in range(0, width, HEAD_DIM):
            low, high = which * width + at, which * width + at + HEAD_DIM
            x = pre_ref[:, low:high] * factor * gain_ref[:, low:high]
            x = x * cosine + pltpu.roll(x, HEAD_DIM // 2, 1) * sine
            out_ref[:, at : at + HEAD_DIM] = x.astype(bf16)
    v_ref[...] = pre_ref[:, 2 * width :].astype(bf16)


def prep(pre, square, gains, cosine, sine):
    rows, triple = pre.shape
    width = triple // 3
    step = 512
    return pl.pallas_call(
        prep_kernel,
        grid=(rows // step,),
        in_specs=[
            pl.BlockSpec((step, triple), lambda i: (i, 0)),
            pl.BlockSpec((2, step), lambda i: (0, i)),
            pl.BlockSpec((1, 2 * width), lambda i: (0, 0)),
            pl.BlockSpec((step, HEAD_DIM), lambda i: (i, 0)),
            pl.BlockSpec((step, HEAD_DIM), lambda i: (i, 0)),
        ],
        out_specs=[pl.BlockSpec((step, width), lambda i: (i, 0))] * 3,
        out_shape=[jax.ShapeDtypeStruct((rows, width), bf16)] * 3,
        cost_estimate=pl.CostEstimate(
            flops=rows * triple * 8, bytes_accessed=rows * triple * 6, transcendentals=0
        ),
        name="prep",
    )(pre, square, gains, cosine, sine)


def attend_kernel(starts_ref, q_ref, k_ref, v_ref, low_ref, mixed_ref, total_ref):
    at = pl.program_id(1)
    query = q_ref[...]
    rows = query.shape[0]

    def step(carry, key_start, key_count, masked):
        row_max, row_sum, mixed = carry
        key = k_ref[pl.ds(key_start, key_count), :]
        value = v_ref[pl.ds(key_start, key_count), :]
        scores = against(query, key) * score_factor
        if masked:
            allowed = allowed_block(starts_ref, at * rows, rows, key_start, key_count)
            scores = jnp.where(allowed, scores, masked_score)
        new_max = jnp.maximum(row_max, jnp.max(scores, axis=1, keepdims=True))
        fade = jnp.exp(row_max - new_max)
        exponent = jnp.exp(scores - new_max)
        row_sum = row_sum * fade + jnp.sum(exponent, axis=1, keepdims=True)
        mixed = mixed * fade + matmul(exponent.astype(bf16), value)
        return new_max, row_sum, mixed

    carry = (
        jnp.full((rows, 1), masked_score, f32),
        jnp.zeros((rows, 1), f32),
        jnp.zeros((rows, HEAD_DIM), f32),
    )
    carry = step(carry, pl.multiple_of(at * rows, rows), rows, True)
    carry = lax.fori_loop(
        0,
        at,
        lambda j, c: step(c, pl.multiple_of(j * rows, rows), rows, False),
        carry,
    )
    edge = (at + 1) * rows
    carry = lax.fori_loop(
        0,
        straddles(starts_ref, edge),
        lambda j, c: step(c, pl.multiple_of(edge, rows), PIECE, True),
        carry,
    )
    row_max, row_sum, mixed = carry
    mixed = mixed / row_sum
    low_ref[...] = mixed.astype(bf16)
    mixed_ref[...] = mixed
    total_ref[...] = jnp.broadcast_to(row_max + jnp.log(row_sum), (rows, HEAD_DIM))


def attend(starts, query, key, value):
    rows, width = query.shape
    heads = width // HEAD_DIM
    block = pl.BlockSpec((BLOCK, HEAD_DIM), lambda h, i, s: (i, h))
    column = pl.BlockSpec((rows, HEAD_DIM), lambda h, i, s: (0, h))
    return pl.pallas_call(
        attend_kernel,
        grid_spec=pltpu.PrefetchScalarGridSpec(
            num_scalar_prefetch=1,
            grid=(heads, rows // BLOCK),
            in_specs=[block, column, column],
            out_specs=[block, block, block],
        ),
        out_shape=[
            jax.ShapeDtypeStruct((rows, width), bf16),
            jax.ShapeDtypeStruct((rows, width), f32),
            jax.ShapeDtypeStruct((rows, width), f32),
        ],
        cost_estimate=pl.CostEstimate(
            flops=heads * rows * rows * HEAD_DIM * 2,
            bytes_accessed=rows * width * 16,
            transcendentals=heads * rows * rows // 2,
        ),
        name="attend",
    )(starts, query, key, value)


def attend_back_kernel(
    starts_ref,
    q_ref,
    grad_ref,
    mixed_ref,
    total_ref,
    k_ref,
    v_ref,
    cos_ref,
    sin_ref,
    dq_ref,
    dk_ref,
    dv_ref,
    dv_total,
):
    at = pl.program_id(1)
    query = q_ref[...]
    grad = grad_ref[...]
    rows = query.shape[0]
    total = total_ref[:, 0:1]
    inner = jnp.sum(grad.astype(f32) * mixed_ref[...], axis=1, keepdims=True)

    @pl.when(at == 0)
    def _():
        dk_ref[...] = jnp.zeros_like(dk_ref)
        dv_total[...] = jnp.zeros_like(dv_total)

    def step(dq, key_start, key_count, masked):
        here = pl.ds(key_start, key_count)
        key = k_ref[here, :]
        value = v_ref[here, :]
        scores = against(query, key) * score_factor
        if masked:
            allowed = allowed_block(starts_ref, at * rows, rows, key_start, key_count)
            scores = jnp.where(allowed, scores, masked_score)
        shares = jnp.exp(scores - total)
        share_grad = against(grad, value)
        score_grad = (shares * (share_grad - inner)).astype(bf16)
        dk_ref[here, :] += across(score_grad, query)
        dv_total[here, :] += across(shares.astype(bf16), grad)
        return dq + matmul(score_grad, key)

    dq = jnp.zeros((rows, HEAD_DIM), f32)
    dq = step(dq, pl.multiple_of(at * rows, rows), rows, True)
    dq = lax.fori_loop(
        0, at, lambda j, c: step(c, pl.multiple_of(j * rows, rows), rows, False), dq
    )
    edge = (at + 1) * rows
    dq = lax.fori_loop(
        0,
        straddles(starts_ref, edge),
        lambda j, c: step(c, pl.multiple_of(edge, rows), PIECE, True),
        dq,
    )

    def unrotated(x, cosine, sine):
        x = x * score_factor
        return x * cosine - pltpu.roll(x, HEAD_DIM // 2, 1) * sine

    mine = pl.ds(pl.multiple_of(at * rows, rows), rows)
    dq_ref[...] = unrotated(dq, cos_ref[mine, :], sin_ref[mine, :])

    @pl.when(at == pl.num_programs(1) - 1)
    def _():
        dk_ref[...] = unrotated(dk_ref[...], cos_ref[...], sin_ref[...])
        dv_ref[...] = dv_total[...].astype(bf16)


def attend_back(starts, query, grad, mixed, total, key, value, cosine, sine):
    rows, width = query.shape
    heads = width // HEAD_DIM
    block = pl.BlockSpec((BLOCK, HEAD_DIM), lambda h, i, s: (i, h))
    column = pl.BlockSpec((rows, HEAD_DIM), lambda h, i, s: (0, h))
    table = pl.BlockSpec((rows, HEAD_DIM), lambda h, i, s: (0, 0))
    return pl.pallas_call(
        attend_back_kernel,
        grid_spec=pltpu.PrefetchScalarGridSpec(
            num_scalar_prefetch=1,
            grid=(heads, rows // BLOCK),
            in_specs=[block, block, block, block, column, column, table, table],
            out_specs=[block, column, column],
            scratch_shapes=[pltpu.VMEM((rows, HEAD_DIM), f32)],
        ),
        out_shape=[
            jax.ShapeDtypeStruct((rows, width), f32),
            jax.ShapeDtypeStruct((rows, width), f32),
            jax.ShapeDtypeStruct((rows, width), bf16),
        ],
        cost_estimate=pl.CostEstimate(
            flops=heads * rows * rows * HEAD_DIM * 5,
            bytes_accessed=rows * width * 28,
            transcendentals=heads * rows * rows // 2,
        ),
        name="attend_back",
    )(starts, query, grad, mixed, total, key, value, cosine, sine)


def body(
    tokens,
    query_weight,
    key_weight,
    value_weight,
    query_norm,
    key_norm,
    output_weight,
    mixer_norm,
    gate_weight,
    up_weight,
    down_weight,
    feeder_norm,
    piece_starts,
    cotangent,
):
    own_rows, model_width = tokens.shape
    group = lax.axis_size("fsdp")
    assert lax.axis_size("rep") == 4 and group % 4 == 0
    me = lax.axis_index("fsdp")
    chain = SEQ // own_rows
    spot = me % chain
    width = model_width // chain
    shard = model_width // group
    part = shard // 4
    sequence = ((lax.axis_index("rep") * group + me) * own_rows) // SEQ
    starts = lax.dynamic_index_in_dim(piece_starts, sequence, 0, keepdims=False)
    teams = None
    if group != chain:
        teams = [[b * chain + i for i in range(chain)] for b in range(group // chain)]
    strides = [[r + 4 * m for m in range(group // 4)] for r in range(4)]

    def of_sequence(block):
        return lax.all_gather(block, "fsdp", axis=0, tiled=True, axis_index_groups=teams)

    def to_sequence_rows(block):
        return lax.psum_scatter(
            block.astype(bf16),
            "fsdp",
            scatter_dimension=0,
            tiled=True,
            axis_index_groups=teams,
        ).astype(f32)

    def to_group_rows(block):
        return lax.psum_scatter(
            block.astype(bf16), "fsdp", scatter_dimension=0, tiled=True
        ).astype(f32)

    def exchanged(block):
        return lax.all_to_all(block, "fsdp", 0, 0, axis_index_groups=teams)

    def of_quad(block):
        half = block.shape[0] // 2
        along_y = swapped(block, "fsdp", 1)
        along_z = swapped(block, "fsdp", 2)
        top = swapped(along_y[:half], "fsdp", 2)
        bottom = swapped(along_z[half:], "fsdp", 1)
        return jnp.concatenate([block, along_y, along_z, top, bottom])

    def to_quad_rows(terms, fill=None):
        half = own_rows // 2
        across_rows = terms(3 * own_rows, 4 * own_rows).astype(bf16)
        top = swapped(across_rows[:half], "fsdp", 2)
        bottom = swapped(across_rows[half:], "fsdp", 1)
        middle = terms(own_rows, 3 * own_rows)
        y_rows = jnp.concatenate(
            [middle[:half] + top.astype(f32), middle[half:own_rows]]
        ).astype(bf16)
        z_rows = jnp.concatenate(
            [
                middle[own_rows : own_rows + half],
                middle[own_rows + half :] + bottom.astype(f32),
            ]
        ).astype(bf16)
        from_y = swapped(y_rows, "fsdp", 1)
        from_z = swapped(z_rows, "fsdp", 2)
        own = terms(0, own_rows, y_rows, z_rows)
        if fill is not None:
            from_y = after(from_y, *fill(own))
        return own + from_y.astype(f32) + from_z.astype(f32)

    def widened(weight, first, second):
        if group != 8:
            return lax.all_gather(
                weight, "fsdp", axis=1, tiled=True, axis_index_groups=strides
            )
        mine = after(own_part(weight, 4, 0, 1), first)
        theirs = swapped(mine, "fsdp", 4)
        theirs = shared(after(theirs, second))
        blocks = []
        for v in (0, 2, 1, 3):
            blocks += [own_part(weight, 4, v, 1), theirs[v]]
        return jnp.concatenate(blocks, axis=1)

    def replica_columns(pieces):
        size = pieces[0].shape[1]
        whole = jnp.zeros((pieces[0].shape[0], 4 * size), f32)
        for v, block in enumerate(pieces):
            start = (lax.axis_index("rep") ^ v) * size
            whole = lax.dynamic_update_slice_in_dim(whole, block.astype(f32), start, 1)
        return whole

    def send_terms(rows, units):
        return across(rows, units[:, units.shape[1] // 2 :]).astype(bf16)

    def keep_terms(rows, units, near):
        total = across(rows, units[:, : units.shape[1] // 2]) + near.astype(f32)
        half = total.shape[1] // 2
        return total[:, :half], total[:, half:].astype(bf16)

    def to_partner(kept, far):
        total = kept + far.astype(f32)
        half = total.shape[1] // 2
        return total[:, :half], total[:, half:].astype(bf16)

    def narrowed_whole(rows, units):
        total = lax.psum_scatter(
            across(rows, units).astype(bf16),
            "fsdp",
            scatter_dimension=1,
            tiled=True,
            axis_index_groups=strides,
        )
        return lax.psum(total, "rep").astype(f32)

    half = HEAD_DIM // 2
    frequency = rope_base ** (-(jnp.arange(half, dtype=f32) * (2.0 / HEAD_DIM)))
    angles = jnp.arange(SEQ, dtype=jnp.int32).astype(f32)[:, None] * frequency[None, :]
    cosine, sine = jnp.cos(angles), jnp.sin(angles)
    cosine = jnp.concatenate([cosine, cosine], axis=1)
    sine = jnp.concatenate([-sine, sine], axis=1)

    rows_weight = jnp.stack(
        [own_part(w, 4, 0, 0) for w in (query_weight, key_weight, value_weight)], axis=1
    )
    rows_weight = rows_weight.reshape(part, 3, chain, width).transpose(2, 0, 1, 3)
    rows_weight = rows_weight.reshape(chain, part, 3 * width)
    if group != chain:
        rows_weight = jnp.tile(rows_weight, (group // chain, 1, 1))
    columns_weight = lax.all_to_all(rows_weight, "fsdp", 0, 0)
    column_slots = shared(columns_weight)
    triple_weight = jnp.stack(in_order(column_slots), axis=1)
    triple_weight = triple_weight.reshape(model_width, 3 * width)
    all_tokens = of_sequence(tokens)

    own_gains = jnp.stack([query_norm, key_norm, mixer_norm, feeder_norm]).astype(f32)
    gains = lax.dynamic_update_slice_in_dim(
        jnp.zeros((4, model_width), f32), own_gains, me * shard, 1
    )
    if group == chain:
        pair_gains = own_gains[:2]
    else:
        gains = xor_sum(gains, "fsdp", group)
        pair_gains = lax.dynamic_slice_in_dim(gains[:2], spot * width, width, 1)

    pre = matmul(all_tokens, triple_weight)
    query_pre, key_pre = pre[:, :width], pre[:, width : 2 * width]
    squares = jnp.stack(
        [jnp.sum(query_pre * query_pre, axis=1), jnp.sum(key_pre * key_pre, axis=1)]
    )
    if group == chain:
        packed = xor_sum(
            jnp.concatenate([squares.reshape(-1, model_width), gains]), "fsdp", group
        )
        squares, gains = packed[:-4].reshape(2, -1), packed[-4:]
    else:
        squares = xor_sum(squares, "fsdp", chain)
    mixer_gain = gains[2:3]
    feeder_gain = gains[3:4]
    query_low, key_low, value_low = prep(
        pre, squares, pair_gains.reshape(1, 2 * width), cosine, sine
    )
    mixed_low, mixed, log_total = attend(starts, query_low, key_low, value_low)
    output_piece = lax.all_gather(
        after(own_part(output_weight, 4, 0, 1), squares), "fsdp", axis=0, tiled=True
    )
    output_piece = after(output_piece, mixed_low)
    output_slots = shared(output_piece)
    whole_output = jnp.concatenate([output_slots[v] for v in (0, 2, 1, 3)], axis=1)

    mixed_rows = exchanged(mixed_low.reshape(chain, own_rows, width))
    mixed_rows = mixed_rows.transpose(1, 0, 2).reshape(own_rows, model_width)
    branch_near = matmul(mixed_rows, whole_output)
    quarter = model_width // 4
    branch_slots = [branch_near[:, i * quarter : (i + 1) * quarter] for i in (0, 2, 1, 3)]
    branch_pre = jnp.concatenate(in_order(branch_slots), axis=1)
    branch_factor = inverse_rms(branch_pre)
    hidden = tokens.astype(f32) + branch_pre * branch_factor * mixer_gain

    wide_gate = widened(gate_weight, mixed_low, branch_near)
    wide_up = widened(up_weight, mixed_rows, branch_near)
    all_hidden = of_quad(hidden.astype(bf16))
    gate = matmul(all_hidden, wide_gate).astype(bf16)
    wide_down = widened(down_weight, mixed_rows, gate)
    up = matmul(all_hidden, wide_up).astype(bf16)
    gate_wide, up_wide = gate.astype(f32), up.astype(f32)
    sigmoid = jax.nn.sigmoid(gate_wide)
    inner = (gate_wide * sigmoid * up_wide).astype(bf16)

    def down_terms(low, high, *deps):
        return against(after(inner[low:high], *deps), wide_down)

    down_pre = to_quad_rows(down_terms)
    down_factor = inverse_rms(down_pre)
    result = (hidden + down_pre * down_factor * feeder_gain).astype(bf16)

    tangent = cotangent.astype(f32)
    feeder_part = jnp.sum(tangent * down_pre * down_factor, axis=0)
    down_grad = norm_backward(down_pre, down_factor, feeder_gain, tangent).astype(bf16)
    all_down_grad = of_quad(down_grad)
    if group == 8:
        down_send = send_terms(all_down_grad, inner)
        down_near = swapped(down_send, "rep", 1)
        inner_grad = matmul(after(all_down_grad, down_send), wide_down)
    else:
        inner_grad = matmul(all_down_grad, wide_down)
    gate_grad = (
        inner_grad * up_wide * sigmoid * (1.0 + gate_wide * (1.0 - sigmoid))
    ).astype(bf16)
    up_grad = (inner_grad * gate_wide * sigmoid).astype(bf16)
    if group == 8:
        down_kept, down_pass = keep_terms(
            all_down_grad, after(inner, gate_grad, up_grad), down_near
        )
        down_far = swapped(down_pass, "rep", 2)
        back_gate, back_up = after(gate_grad, down_pass), after(up_grad, down_pass)
    else:
        back_gate, back_up = gate_grad, up_grad
    stage = {}

    def early_gradients(own):
        if group != 8:
            return ()
        late_gate = after(gate_grad, own)
        gate_send = send_terms(all_hidden, late_gate)
        gate_near = swapped(gate_send, "rep", 1)
        up_send = send_terms(all_hidden, after(up_grad, gate_send))
        stage["up_near"] = swapped(up_send, "rep", 1)
        gate_kept, gate_pass = keep_terms(
            all_hidden, after(gate_grad, up_send), gate_near
        )
        stage["gate"] = gate_kept, swapped(gate_pass, "rep", 2)
        kept, passed = to_partner(down_kept, after(down_far, gate_pass))
        stage["down"] = kept, swapped(passed, "fsdp", 4)
        return (gate_pass, passed)

    def back_terms(low, high, *deps):
        return against(after(back_gate[low:high], *deps), wide_gate) + against(
            after(back_up[low:high], *deps), wide_up
        )

    feed_back = to_quad_rows(back_terms, early_gradients)
    hidden_grad = tangent + feed_back
    mixer_part = jnp.sum(hidden_grad * branch_pre * branch_factor, axis=0)
    branch_grad = norm_backward(
        branch_pre, branch_factor, mixer_gain, hidden_grad
    ).astype(bf16)

    grad_near = jnp.concatenate(
        [own_part(branch_grad, 4, v, 1) for v in (0, 2, 1, 3)], axis=1
    )
    mixed_grad_rows = against(grad_near, whole_output).astype(bf16)
    mixed_grad_rows = mixed_grad_rows.reshape(own_rows, chain, width).transpose(1, 0, 2)
    mixed_grad = exchanged(mixed_grad_rows)
    mixed_grad = mixed_grad.reshape(chain * own_rows, width)
    output_half = model_width // 2
    late_rows = after(mixed_rows, mixed_grad_rows)
    output_send = across(late_rows, grad_near[:, output_half:]).astype(bf16)
    output_near = swapped(output_send, "rep", 1)
    late_rows = after(mixed_rows, output_send)
    if group == 8:
        late_up = after(up_grad, output_send)
        up_kept, up_pass = keep_terms(all_hidden, late_up, stage["up_near"])
        up_far = swapped(up_pass, "rep", 2)
        late_rows = after(mixed_rows, up_pass)
    output_kept = across(late_rows, grad_near[:, :output_half]) + output_near.astype(f32)
    output_pass = output_kept[:, quarter:].astype(bf16)
    output_kept = output_kept[:, :quarter]
    output_far = swapped(output_pass, "rep", 2)
    if group == 8:
        down_first, down_theirs = stage["down"]
        gate_kept, gate_far = stage["gate"]
        gate_kept, gate_pass = to_partner(gate_kept, after(gate_far, mixed_grad))
        gate_theirs = swapped(gate_pass, "fsdp", 4)
        mixed_grad = after(mixed_grad, output_pass)
    query_turn, key_turn, value_grad = attend_back(
        starts,
        query_low,
        mixed_grad,
        mixed,
        log_total,
        key_low,
        value_low,
        cosine,
        sine,
    )
    query_gain, key_gain = pair_gains[0:1], pair_gains[1:2]
    means = jnp.stack(
        [
            jnp.sum(query_gain * query_turn * query_pre, axis=1),
            jnp.sum(key_gain * key_turn * key_pre, axis=1),
        ]
    )
    factors = lax.rsqrt(squares * (1.0 / model_width) + norm_epsilon)

    def gain_part(turn, pre_part, at):
        own = jnp.sum(turn * pre_part * factors[at][:, None], axis=0)
        whole = jnp.zeros((model_width,), f32)
        return lax.dynamic_update_slice_in_dim(whole, own, spot * width, 0)

    gain_parts = jnp.stack(
        [
            gain_part(query_turn, query_pre, 0),
            gain_part(key_turn, key_pre, 1),
            mixer_part,
            feeder_part,
        ]
    )
    if group == chain and model_width == means.shape[1]:
        packed = xor_sum(jnp.concatenate([means, gain_parts]), "fsdp", group)
        means, gain_parts = packed[:2], packed[2:]
    else:
        means = xor_sum(means, "fsdp", chain)
        gain_parts = xor_sum(gain_parts, "fsdp", group)
    means = means * (1.0 / model_width)

    def pair_back(turn, pre_part, gain, at):
        factor = factors[at][:, None]
        grad = factor * gain * turn - pre_part * factor * factor * factor * means[at][:, None]
        return grad.astype(bf16)

    query_grad = pair_back(query_turn, query_pre, query_gain, 0)
    key_grad = pair_back(key_turn, key_pre, key_gain, 1)
    triple_grad = jnp.concatenate([query_grad, key_grad, value_grad], axis=1)
    if group == 8:
        down_total = (
            down_first + after(down_theirs, triple_grad).astype(f32)
        ).astype(bf16)
        down_pieces = shared(down_total)
    token_terms = against(triple_grad, triple_weight).astype(bf16)
    token_rows = to_sequence_rows(token_terms)
    gradient_tokens = (hidden_grad + token_rows).astype(bf16)

    late_grad = after(triple_grad, token_terms)
    triple_part = across(all_tokens, late_grad)
    if group == chain:
        triple_part = triple_part.reshape(chain, 4, part, 3 * width)
        slots = [own_part(triple_part, 4, v, 1)[:, 0] for v in range(4)]
        sends = [slots[v].astype(bf16) for v in (3, 1)]
        near = [swapped(x, "rep", 1) for x in sends]
        passed = (slots[2] + near[0].astype(f32)).astype(bf16)
        kept = slots[0] + near[1].astype(f32)
        passed_far = swapped(passed, "rep", 2)
        if group == 8:
            up_kept, up_pass = to_partner(up_kept, after(up_far, passed))
            up_theirs = swapped(up_pass, "fsdp", 4)
            output_far = after(output_far, up_pass)
        output_terms = (output_kept + output_far.astype(f32)).astype(bf16)
        output_part = lax.all_to_all(
            output_terms.reshape(group, shard, quarter), "fsdp", 0, 0
        )
        output_part = jnp.sum(output_part.astype(f32), axis=0).astype(bf16)
        passed_far = after(passed_far, output_terms)
        kept = (kept + passed_far.astype(f32)).astype(bf16)
        heads_rows = lax.all_to_all(kept, "fsdp", 0, 0)
        if group == 8:
            gate_theirs = after(gate_theirs, kept)
            gate_total = (gate_kept + gate_theirs.astype(f32)).astype(bf16)
            gate_pieces = shared(gate_total)
            heads_rows = after(heads_rows, gate_total)
        triple_pieces = shared(heads_rows)
        if group == 8:
            up_theirs = after(up_theirs, heads_rows)
            up_total = (up_kept + up_theirs.astype(f32)).astype(bf16)
            up_pieces = shared(up_total)
            output_part = after(output_part, up_total)
            gradient_down = replica_columns(down_pieces)
            gradient_gate = replica_columns(gate_pieces)
            gradient_up = replica_columns(up_pieces)
        output_pieces = shared(output_part)
        triple_rows = jnp.stack(in_order(triple_pieces))
        triple_rows = triple_rows.reshape(4, chain, part, 3, width)
        triple_rows = triple_rows.transpose(3, 0, 2, 1, 4).reshape(3, shard, model_width)
    else:
        output_terms = (output_kept + output_far.astype(f32)).astype(bf16)
        output_pieces = shared(to_group_rows(output_terms).astype(bf16))
        triple_rows = lax.dynamic_update_slice_in_dim(
            jnp.zeros((model_width, 3, chain, width), f32),
            triple_part.reshape(model_width, 3, 1, width),
            spot,
            2,
        )
        triple_rows = to_group_rows(triple_rows.reshape(model_width, 3 * model_width))
        triple_rows = lax.psum(triple_rows.astype(bf16), "rep")
        triple_rows = triple_rows.reshape(shard, 3, model_width).transpose(1, 0, 2)
    gradient_output = replica_columns(output_pieces)
    if group != 8:
        gradient_down = narrowed_whole(all_down_grad, inner)
        gradient_gate = narrowed_whole(all_hidden, gate_grad)
        gradient_up = narrowed_whole(all_hidden, up_grad)
    triple_rows = triple_rows.astype(f32)

    gain_parts = xor_sum(gain_parts, "rep", 4)
    gain_own = lax.dynamic_slice_in_dim(gain_parts, me * shard, shard, 1)
    return (
        result,
        gradient_tokens,
        triple_rows[0],
        triple_rows[1],
        triple_rows[2],
        gain_own[0],
        gain_own[1],
        gradient_output,
        gain_own[2],
        gradient_gate,
        gradient_up,
        gradient_down,
        gain_own[3],
    )


def solution(mesh):
    rows, ends = P(("rep", "fsdp"), None), P(None, "fsdp")
    tops, line = P("fsdp", None), P("fsdp")
    return jax.shard_map(
        body,
        mesh=mesh,
        in_specs=(
            rows, tops, tops, tops, line, line, tops, line, ends, ends, ends, line, P(), rows,
        ),
        out_specs=(
            rows, rows, tops, tops, tops, line, line, tops, line, ends, ends, ends, line,
        ),
        check_vma=False,
    )
```
